32 devices in a mesh: row: 4 (over y, core), col: 8 (over z, x).
Axes of the slice: x: 2, y: 2, z: 4, core: 2. Of those that a mesh axis runs over, the one named last changes fastest.
Arguments:
- covariance: float32 [9216, 9216], P('row', 'col'), may hold values from -1 to 10, as said below
- samples: float32 [192, 9216], P(None, ('col', 'row')), may hold values from -2 to 2
- labels: int32 [192], replicated, may hold values from 0 to 1023
- weights: float32 [9216, 1024], P(('col', 'row')), may hold values from -2.5 to 2.5
Outputs:
- new_covariance: float32 [9216, 9216], P('row', 'col')
- new_weights: float32 [9216, 1024], P(('col', 'row'))
The draws below stay inside these ranges and needn't reach their ends.
Inputs may be any that keep to these rules, and one draw needn't show every extreme that they name: covariance is symmetric and positive definite.
All inputs are finite; a program needn't handle non-finite values.
Results may differ from the reference program's by a relative error of at most 0.00005.
Values sent between devices are 32-bit elements; how exact they have to be, the bound alone decides.
No kernel may reach another device: no remote copies, remote signals or barrier semaphores. Data moves between devices by JAX's collectives and lax.ppermute only.
A program may use at most 64 MiB of HBM per device.

```python
import math
import jax
import jax.numpy as jnp
from jax import lax

D = 9216
CLASSES = 1024
SAMPLES = 192


def draw_covariance(key, part):
    normals = jax.random.normal(key, (D, D), jnp.float32)
    noise = (normals + normals.T) * (0.4 / math.sqrt(2.0 * D))
    matrix = noise + jnp.eye(D, dtype=jnp.float32)
    return matrix


def draw_samples(key, part):
    spread = math.sqrt(8.0 / D)
    normals = jnp.clip(jax.random.normal(jax.random.fold_in(key, 11), (SAMPLES, D), jnp.float32), -6.0, 6.0)
    row_scales = jnp.exp(jax.random.uniform(jax.random.fold_in(key, 13), (SAMPLES,), jnp.float32, -2.0, 1.0))
    return normals * spread * row_scales[:, None]


def with_ends(array, stream_key, least, high):
    longest = array.shape.index(max(array.shape))
    spots = []
    for shift in (0, 1):
        where = [jax.random.randint(jax.random.fold_in(stream_key, axis), (), 0, length) for axis, length in enumerate(array.shape)]
        where[longest] = (where[longest] + shift) % array.shape[longest]
        spots.append(tuple(where))
    return array.at[spots[0]].set(least).at[spots[1]].set(high)


def steps_of(rng, shape, split, smallest, high):
    level, own = 1.0, jax.random.fold_in(rng, 6)
    for position, blocks in split:
        steps = jnp.exp(jax.random.uniform(jax.random.fold_in(own, position), (blocks,), jnp.float32, smallest / len(split), high / len(split)))
        level = level * jnp.repeat(steps, shape[position] // blocks).reshape([-1 if axis == position else 1 for axis in range(len(shape))])
    return level


def gaussian(stream_key, dims, scale, bound, split=(), kind=jnp.bfloat16):
    array = scale * jax.random.normal(stream_key, dims, jnp.float32)
    if split:
        array = array * steps_of(stream_key, dims, split, -0.22, 0.18)
    return jnp.clip(array, -bound, bound).astype(kind)


def setup_inputs(seed: int = 0) -> dict:
    streams_of = jax.random.split(jax.random.key(seed), 5)
    return {
        "covariance": draw_covariance(jax.random.fold_in(streams_of[4], 71), 0),
        "samples": draw_samples(jax.random.fold_in(streams_of[4], 71), 0),
        "labels": with_ends(jax.random.randint(streams_of[2], (SAMPLES,), 0, CLASSES), jax.random.fold_in(streams_of[2], 1), 0, CLASSES - 1).astype(jnp.int32),
        "weights": gaussian(streams_of[3], (D, CLASSES), 0.35, 2.5, ((0, 32),), jnp.float32),
    }


def reference(covariance, samples, labels, weights):
    precise = lax.Precision.HIGHEST
    products = jnp.dot(samples.astype(jnp.float32), covariance.astype(jnp.float32), precision=precise, preferred_element_type=jnp.float32)
    inner = jnp.dot(samples.astype(jnp.float32), products.T.astype(jnp.float32), precision=precise, preferred_element_type=jnp.float32)
    innovation = 0.5 * (inner + inner.T) + jnp.eye(SAMPLES, dtype=jnp.float32)
    factor = jnp.linalg.cholesky(innovation)
    gain = jax.scipy.linalg.cho_solve((factor, True), products)
    new_covariance = covariance - jnp.dot(products.T.astype(jnp.float32), gain.astype(jnp.float32), precision=precise, preferred_element_type=jnp.float32)
    classes = lax.broadcasted_iota(jnp.int32, (SAMPLES, CLASSES), 1)
    targets = (labels[:, None] == classes).astype(jnp.float32)
    predicted = jnp.dot(samples.astype(jnp.float32), weights.astype(jnp.float32), precision=precise, preferred_element_type=jnp.float32)
    new_weights = weights + jnp.dot(gain.T.astype(jnp.float32), (targets - predicted).astype(jnp.float32), precision=precise, preferred_element_type=jnp.float32)
    return (new_covariance, new_weights)
```

```python
import jax
import jax.numpy as jnp
from jax import lax
from jax.sharding import PartitionSpec as P


HIGHEST = lax.Precision.HIGHEST
HIGH = lax.Precision.HIGH


def dot(a, b, dims, precision=HIGHEST):
    return lax.dot_general(
        a, b, ((dims[:1], dims[1:]), ((), ())), precision=precision, preferred_element_type=jnp.float32
    )


def program(nr, nc):
    k = nc // nr

    def swap(a, axis, mask):
        n = nr if axis == "row" else nc
        return lax.ppermute(a, axis, [(i, i ^ mask) for i in range(n)])

    def bits_of(n):
        return [1 << b for b in range(n.bit_length() - 1)]

    def on_device(covariance, samples, labels, weights):
        row, col = lax.axis_index("row"), lax.axis_index("col")
        z, x = col // k, col % k
        batch, piece = samples.shape
        half = covariance.shape[0] // k

        def own(index, mask):
            return (index & mask) == 0

        def ordered(low, mine, other):
            return jnp.where(low, mine, other), jnp.where(low, other, mine)

        xt = samples.T
        transposed = [
            (z_ * nc + k * r_ + x_, r_ * nc + k * z_ + x_) for r_ in range(nr) for z_ in range(nr) for x_ in range(k)
        ]
        x_piece = lax.ppermute(xt, ("row", "col"), transposed)
        x_cols = xt
        for mask in reversed(bits_of(nr)):
            x_cols = jnp.stack(ordered(own(row, mask), x_cols, swap(x_cols, "row", mask)), axis=-3)
        x_cols = x_cols.reshape(nr * piece, batch)

        predicted = dot(samples, weights, (1, 0))
        steps = [("row", row, m) for m in bits_of(nr)] + [("col", col, m) for m in bits_of(k)]
        for axis, index, mask in steps:
            n = predicted.shape[0] // 2
            low = own(index, mask)
            a, b = predicted[:n], predicted[n:]
            predicted = jnp.where(low, a, b) + swap(jnp.where(low, b, a), axis, mask)
        for mask in bits_of(nr):
            predicted = predicted + swap(predicted, "col", mask * k)
        for axis, index, mask in reversed(steps):
            predicted = jnp.concatenate(ordered(own(index, mask), predicted, swap(predicted, axis, mask)))

        terms = dot(covariance, x_cols, (1, 0), HIGH)
        for mask in bits_of(k):
            n = terms.shape[0] // 2
            low = own(x, mask)
            a, b = terms[:n], terms[n:]
            terms = jnp.where(low, a, b) + swap(jnp.where(low, b, a), "col", mask)
        assert k == 2

        def turned(s):
            return [(z_ * k + x_, (z_ + s) % nr * k + x_) for z_ in range(nr) for x_ in range(k)]

        def part(a, index):
            return lax.dynamic_slice_in_dim(a, index * piece, piece, 0)

        u_piece = part(terms, z)
        for s in range(1, nr):
            u_piece = u_piece + lax.ppermute(part(terms, (z + s) % nr), "col", turned(s))

        inner = dot(u_piece, x_piece, (0, 0))
        for mask in bits_of(nr):
            inner = inner + swap(inner, "row", mask)
        for mask in bits_of(nc):
            inner = inner + swap(inner, "col", mask)

        block = jnp.zeros((nr * piece, batch), jnp.float32)
        block = lax.dynamic_update_slice_in_dim(block, u_piece, z * piece, 0)
        for s in range(1, nr):
            got = lax.ppermute(u_piece, "col", turned(s))
            block = lax.dynamic_update_slice_in_dim(block, got, (z - s) % nr * piece, 0)
        u_rows = jnp.concatenate(ordered(own(x, 1), block, swap(block, "col", 1)))
        u_cols = block
        for mask in bits_of(nr):
            got = swap(u_cols, "row", mask)
            u_cols = jnp.where((row ^ z) & ~(mask - 1) & mask != 0, got, u_cols)

        innovation = 0.5 * (inner + inner.T) + jnp.eye(batch, dtype=jnp.float32)
        factor = jnp.linalg.cholesky(innovation)
        inverse = jax.scipy.linalg.cho_solve((factor, True), jnp.eye(batch, dtype=jnp.float32))
        gain = dot(u_cols, inverse, (1, 0))
        new_covariance = covariance - dot(u_rows, gain, (1, 1), HIGH)
        classes = lax.broadcasted_iota(jnp.int32, (batch, weights.shape[1]), 1)
        targets = (labels[:, None] == classes).astype(jnp.float32)
        new_weights = weights + dot(part(gain, row), targets - predicted, (1, 0))
        return new_covariance, new_weights

    return on_device


def solution(mesh):
    return jax.shard_map(
        program(mesh.shape["row"], mesh.shape["col"]),
        mesh=mesh,
        in_specs=(P("row", "col"), P(None, ("col", "row")), P(), P(("col", "row"), None)),
        out_specs=(P("row", "col"), P(("col", "row"), None)),
        check_vma=False,
    )
```

```python
import functools

import jax
import jax.numpy as jnp
from jax import lax
from jax.experimental import pallas as pl
from jax.experimental.pallas import tpu as pltpu
from jax.sharding import PartitionSpec as P


HIGHEST = lax.Precision.HIGHEST
HIGH = lax.Precision.HIGH
F32, BF16 = jnp.float32, jnp.bfloat16
LANES = 128
PIVOTS = 4
VMEM = pl.BlockSpec(memory_space=pltpu.VMEM)


def dot(a, b, dims, precision=HIGHEST):
    return lax.dot_general(a, b, ((dims[:1], dims[1:]), ((), ())), precision=precision, preferred_element_type=F32)


def halves(a):
    high = a.astype(BF16)
    return high, (a - high.astype(F32)).astype(BF16)


def dot3(a, b, dims):
    (ah, al), (bh, bl) = a, b
    return dot(ah, bh, dims, None) + (dot(ah, bl, dims, None) + dot(al, bh, dims, None))


def packs(n, batch):
    return batch == LANES * 3 // 2 and n % 16 == 0


def pack(a):
    n, batch = a.shape
    if not packs(n, batch):
        return a
    tail = a[:, LANES:]
    return jnp.concatenate([a[:, :LANES], jnp.concatenate([tail[: n // 2], tail[n // 2 :]], axis=1)])


def unpack(a, n, batch):
    if not packs(n, batch):
        return a
    tail = a[n:]
    side = LANES // 2
    return jnp.concatenate([a[:n], jnp.concatenate([tail[:, :side], tail[:, side:]])], axis=1)


def inverse_kernel(s_ref, o_ref, a_ref):
    n, width = a_ref.shape
    s = s_ref[...]
    lane = lax.broadcasted_iota(jnp.int32, (1, width), 1)
    sub = lax.broadcasted_iota(jnp.int32, (n, 1), 0)
    if width > n:
        a_ref[:, n:] = jnp.zeros((n, width - n), F32)
    a_ref[:, :n] = 0.5 * (s + s.T)
    a_ref[...] += jnp.where(sub == lane, 1.0, 0.0)

    def step(t, _):
        first = t * PIVOTS
        a = a_ref[...]
        hits = [lane == first + b for b in range(PIVOTS)]
        rows = [a_ref[pl.ds(first + b, 1), :] for b in range(PIVOTS)]
        p = [[jnp.sum(jnp.where(h, r, 0.0), axis=1, keepdims=True) for h in hits] for r in rows]
        cols = [jnp.sum(jnp.where(h, a, 0.0), axis=1, keepdims=True) for h in hits]
        for i in range(PIVOTS):
            inv = 1.0 / p[i][i]
            scaled = [inv if j == i else p[i][j] * inv for j in range(PIVOTS)]
            for o in range(PIVOTS):
                if o != i:
                    f = p[o][i]
                    p[o] = [-f * inv if j == i else p[o][j] - f * scaled[j] for j in range(PIVOTS)]
            p[i] = scaled
        in_lanes = (lane >= first) & (lane < first + PIVOTS)
        in_rows = (sub >= first) & (sub < first + PIVOTS)
        rows = [jnp.where(in_lanes, jnp.where(h, 1.0, 0.0), r) for h, r in zip(hits, rows)]
        out = jnp.where(in_rows | in_lanes, 0.0, a)
        for i in range(PIVOTS):
            new = p[i][0] * rows[0]
            for j in range(1, PIVOTS):
                new = new + p[i][j] * rows[j]
            out = out - jnp.where(in_rows, jnp.where(sub == first + i, -1.0, 0.0), cols[i]) * new
        a_ref[...] = out
        return 0

    lax.fori_loop(0, n // PIVOTS, step, 0)
    o_ref[...] = a_ref[:, :n]


def inverse_of(inner):
    n = inner.shape[0]
    width = -(-n // LANES) * LANES
    return pl.pallas_call(
        inverse_kernel,
        out_shape=jax.ShapeDtypeStruct((n, n), F32),
        in_specs=[VMEM],
        out_specs=VMEM,
        scratch_shapes=[pltpu.VMEM((n, width), F32)],
        cost_estimate=pl.CostEstimate(flops=2 * n**3, bytes_accessed=8 * n * n, transcendentals=0),
        name="inverse",
    )(inner)


def place_kernel(n, table, *refs):
    *piece_refs, high_ref, low_ref = refs
    for i, ref in enumerate(piece_refs):
        at = pl.ds(pl.multiple_of(table[i] * n, 16), n)
        high_ref[at, :], low_ref[at, :] = halves(unpack(ref[...], n, high_ref.shape[1]))


def placed_halves(pieces, table, n, batch):
    shape = jax.ShapeDtypeStruct((len(pieces) * n, batch), BF16)
    return pl.pallas_call(
        functools.partial(place_kernel, n),
        out_shape=(shape, shape),
        grid_spec=pltpu.PrefetchScalarGridSpec(
            num_scalar_prefetch=1, grid=(), in_specs=[VMEM] * len(pieces), out_specs=(VMEM, VMEM)
        ),
        name="place",
    )(table, *pieces)


def terms_kernel(table, cov_ref, high_ref, low_ref, o_ref):
    o_ref[...] = pack(dot3(halves(cov_ref[...]), (high_ref[...], low_ref[...]), (1, 0)))


def row_terms(covariance, x_high, x_low, blocks, n):
    rows, width = covariance.shape
    batch = x_high.shape[1]
    packed = n * batch // LANES
    count = blocks.shape[0]
    return pl.pallas_call(
        terms_kernel,
        out_shape=jax.ShapeDtypeStruct((count * packed, LANES), F32),
        grid_spec=pltpu.PrefetchScalarGridSpec(
            num_scalar_prefetch=1,
            grid=(count,),
            in_specs=[pl.BlockSpec((n, width), lambda i, t: (t[i], 0)), VMEM, VMEM],
            out_specs=pl.BlockSpec((packed, LANES), lambda i, t: (i, 0)),
        ),
        cost_estimate=pl.CostEstimate(
            flops=6 * count * n * width * batch, bytes_accessed=4 * count * n * width, transcendentals=0
        ),
        name="terms",
    )(blocks, covariance, x_high, x_low)


def gain_kernel(n, table, inverse_ref, *refs):
    *piece_refs, high_ref, low_ref, own_ref = refs
    per = piece_refs[0].shape[0] // (n * inverse_ref.shape[0] // LANES)
    batch = inverse_ref.shape[0]
    size = n * batch // LANES
    for i in range(len(piece_refs) * per):
        packed = piece_refs[i // per][i % per * size : (i % per + 1) * size, :]
        gain = dot(unpack(packed, n, batch), inverse_ref[...], (1, 0))
        at = pl.ds(pl.multiple_of(table[i] * n, 16), n)
        high_ref[at, :], low_ref[at, :] = halves(gain)

        @pl.when(table[i] == table[len(piece_refs) * per])
        def _():
            own_ref[...] = gain


def gain_of(inverse, groups, table, n):
    batch = inverse.shape[0]
    count = table.shape[0] - 1
    shape = jax.ShapeDtypeStruct((count * n, batch), BF16)
    return pl.pallas_call(
        functools.partial(gain_kernel, n),
        out_shape=(shape, shape, jax.ShapeDtypeStruct((n, batch), F32)),
        grid_spec=pltpu.PrefetchScalarGridSpec(
            num_scalar_prefetch=1, grid=(), in_specs=[VMEM] * (1 + len(groups)), out_specs=(VMEM,) * 3
        ),
        name="gain",
    )(table, inverse, *groups)


def update_kernel(n, table, cov_ref, high_ref, low_ref, *refs):
    *group_refs, o_ref, now_ref = refs
    batch = high_ref.shape[1]
    size = n * batch // LANES
    per = group_refs[0].shape[0] // size
    for i in range(len(group_refs) * per):

        @pl.when(pl.program_id(0) == i)
        def _():
            now_ref[...] = group_refs[i // per][i % per * size : (i % per + 1) * size, :]

    rows = halves(unpack(now_ref[...], n, batch))
    o_ref[...] = cov_ref[...] - dot3(rows, (high_ref[...], low_ref[...]), (1, 1))


def updated(covariance, gain_high, gain_low, groups, table, n):
    rows, width = covariance.shape
    batch = gain_high.shape[1]
    size = n * batch // LANES
    block = pl.BlockSpec((n, width), lambda i, t: (t[i], 0))
    return pl.pallas_call(
        functools.partial(update_kernel, n),
        out_shape=jax.ShapeDtypeStruct(covariance.shape, F32),
        grid_spec=pltpu.PrefetchScalarGridSpec(
            num_scalar_prefetch=1,
            grid=(rows // n,),
            in_specs=[block] + [VMEM] * (2 + len(groups)),
            out_specs=block,
            scratch_shapes=[pltpu.VMEM((size, LANES), F32)],
        ),
        name="update",
    )(table, covariance, gain_high, gain_low, *groups)


def program(nr, nc):
    k = nc // nr
    assert k == 2

    def swap(a, axis, mask):
        n = nr if axis == "row" else nc
        return lax.ppermute(a, axis, [(i, i ^ mask) for i in range(n)])

    def bits_of(n):
        return [1 << b for b in range(n.bit_length() - 1)]

    def on_device(covariance, samples, labels, weights):
        row, col = lax.axis_index("row"), lax.axis_index("col")
        z, x = col // k, col % k
        batch, piece = samples.shape
        fits = packs(piece, batch)

        def ordered(low, mine, other):
            return jnp.where(low, mine, other), jnp.where(low, other, mine)

        xt = pack(samples.T)
        size = xt.shape[0]
        x_by = {0: xt}
        for mask in reversed(bits_of(nr)):
            for d in list(x_by):
                x_by[d | mask] = swap(x_by[d], "row", mask)
        transposed = [
            (z_ * nc + k * r_ + x_, r_ * nc + k * z_ + x_) for r_ in range(nr) for z_ in range(nr) for x_ in range(k)
        ]
        x_piece = lax.ppermute(xt, ("row", "col"), transposed)
        offsets = jnp.arange(nr, dtype=jnp.int32)
        by_row = jnp.bitwise_xor(row, offsets)
        by_z = jnp.bitwise_xor(z, offsets)

        predicted = dot(samples, weights, (1, 0))
        steps = [("row", row, m) for m in bits_of(nr)] + [("col", col, m) for m in bits_of(k)]
        for axis, index, mask in steps:
            n = predicted.shape[0] // 2
            low = (index & mask) == 0
            a, b = predicted[:n], predicted[n:]
            predicted = jnp.where(low, a, b) + swap(jnp.where(low, b, a), axis, mask)
        for mask in bits_of(nr):
            predicted = predicted + swap(predicted, "col", mask * k)
        for axis, index, mask in reversed(steps):
            predicted = jnp.concatenate(ordered((index & mask) == 0, predicted, swap(predicted, axis, mask)))

        order = list(reversed(range(nr)))
        groups = [order[: nr // 2], order[nr // 2 :]]
        if fits:
            x_high, x_low = placed_halves([x_by[d] for d in range(nr)], by_row, piece, batch)

            def terms_of(e, group):
                blocks = jnp.bitwise_xor(x, e) * nr + jnp.bitwise_xor(z, jnp.array(group, jnp.int32))
                return row_terms(covariance, x_high, x_low, blocks, piece)
        else:
            x_cols = jnp.concatenate([x_by[0]] * nr)
            for d in range(nr):
                x_cols = lax.dynamic_update_slice_in_dim(x_cols, x_by[d], by_row[d] * piece, 0)
            whole = dot(covariance, x_cols, (1, 0), HIGH)

            def terms_of(e, group):
                at = [(jnp.bitwise_xor(x, e) * nr + jnp.bitwise_xor(z, d)) * piece for d in group]
                return jnp.concatenate([lax.dynamic_slice_in_dim(whole, i, piece, 0) for i in at])

        sent = [swap(terms_of(1, group), "col", 1) for group in groups]
        part = {}
        for group, got in zip(groups, sent):
            kept = terms_of(0, group)
            for i, d in enumerate(group):
                part[d] = kept[i * size : (i + 1) * size] + got[i * size : (i + 1) * size]
        for mask in bits_of(nr):
            for d in sorted(part, reverse=True):
                if d & mask:
                    part[d ^ mask] = part[d ^ mask] + swap(part.pop(d), "col", mask * k)
        u_piece = part[0]

        inner = dot(unpack(u_piece, piece, batch), unpack(x_piece, piece, batch), (0, 0))
        low = (row & 1) == 0
        n = batch // 2
        a, b = inner[:n], inner[n:]
        inner = jnp.where(low, a, b) + swap(jnp.where(low, b, a), "row", 1)
        for mask in bits_of(nr)[1:]:
            inner = inner + swap(inner, "row", mask)
        for mask in bits_of(nc):
            inner = inner + swap(inner, "col", mask)
        inner = jnp.concatenate(ordered(low, inner, swap(inner, "row", 1)))

        u_by = {0: u_piece}
        for mask in reversed(bits_of(nr)):
            for d in list(u_by):
                u_by[d | mask] = swap(u_by[d], "col", mask * k)
        near = sorted(u_by)[: nr // 2]
        far = sorted(u_by)[nr // 2 :]
        own = [jnp.concatenate([u_by[d] for d in part_]) for part_ in (near, far)]
        peer = [swap(a, "col", 1) for a in own]
        u_cols = list(own)
        for mask in reversed(bits_of(nr)):
            pairs = [
                (r_ * nc + c_, (r_ ^ mask) * nc + c_)
                for c_ in range(nc)
                for r_ in range(nr)
                if (r_ ^ (c_ // k)) & (2 * mask - 1) == 0
            ]
            take = (jnp.bitwise_xor(row, z) & mask) != 0
            u_cols = [jnp.where(take, lax.ppermute(a, ("row", "col"), pairs), a) for a in u_cols]

        if fits:
            inverse = inverse_of(inner)
            table = jnp.concatenate([by_z, row[None].astype(jnp.int32)])
            gain_high, gain_low, gain_piece = gain_of(inverse, u_cols, table, piece)
            table = jnp.concatenate([x * nr + by_z, (1 - x) * nr + by_z])
            new_covariance = updated(covariance, gain_high, gain_low, own + peer, table, piece)
        else:

            def in_order(pieces):
                out = jnp.concatenate(pieces)
                for a, group in zip(pieces, (near, far)):
                    for i, d in enumerate(group):
                        got = a[i * piece : (i + 1) * piece]
                        out = lax.dynamic_update_slice_in_dim(out, got, by_z[d] * piece, 0)
                return out

            inverse = inverse_of(inner)
            gain = dot(in_order(u_cols), inverse, (1, 0))
            gain_piece = lax.dynamic_slice_in_dim(gain, row * piece, piece, 0)
            u_rows = jnp.concatenate(ordered(x == 0, in_order(own), in_order(peer)))
            new_covariance = covariance - dot(u_rows, gain, (1, 1), HIGH)
        classes = lax.broadcasted_iota(jnp.int32, (batch, weights.shape[1]), 1)
        targets = (labels[:, None] == classes).astype(F32)
        new_weights = weights + dot(gain_piece, targets - predicted, (1, 0))
        return new_covariance, new_weights

    return on_device


def solution(mesh):
    return jax.shard_map(
        program(mesh.shape["row"], mesh.shape["col"]),
        mesh=mesh,
        in_specs=(P("row", "col"), P(None, ("col", "row")), P(), P(("col", "row"), None)),
        out_specs=(P("row", "col"), P(("col", "row"), None)),
        check_vma=False,
    )
```

```python
import functools

import jax
import jax.numpy as jnp
from jax import lax
from jax.experimental import pallas as pl
from jax.experimental.pallas import tpu as pltpu
from jax.sharding import PartitionSpec as P


HIGHEST = lax.Precision.HIGHEST
HIGH = lax.Precision.HIGH
F32, BF16 = jnp.float32, jnp.bfloat16
LANES = 128
PIVOTS = 4
SMALL = pltpu.CompilerParams(vmem_limit_bytes=20 * 2**20)
VMEM = pl.BlockSpec(memory_space=pltpu.VMEM)


def dot(a, b, dims, precision=HIGHEST):
    return lax.dot_general(a, b, ((dims[:1], dims[1:]), ((), ())), precision=precision, preferred_element_type=F32)


def halves(a):
    high = a.astype(BF16)
    return high, (a - high.astype(F32)).astype(BF16)


def dot3(a, b, dims):
    (ah, al), (bh, bl) = a, b
    return dot(ah, bh, dims, None) + (dot(ah, bl, dims, None) + dot(al, bh, dims, None))


def packs(n, batch):
    return batch == LANES * 3 // 2 and n % 16 == 0


def pack(a):
    n, batch = a.shape
    if not packs(n, batch):
        return a
    tail = a[:, LANES:]
    return jnp.concatenate([a[:, :LANES], jnp.concatenate([tail[: n // 2], tail[n // 2 :]], axis=1)])


def unpack(a, n, batch):
    if not packs(n, batch):
        return a
    tail = a[n:]
    side = LANES // 2
    return jnp.concatenate([a[:n], jnp.concatenate([tail[:, :side], tail[:, side:]])], axis=1)


def inverse_kernel(s_ref, o_ref, a_ref):
    n, width = a_ref.shape
    s = jnp.concatenate([unpack(s_ref[i], n // 2, n) for i in range(2)]) if len(s_ref.shape) == 3 else s_ref[...]
    lane = lax.broadcasted_iota(jnp.int32, (1, width), 1)
    sub = lax.broadcasted_iota(jnp.int32, (n, 1), 0)
    if width > n:
        a_ref[:, n:] = jnp.zeros((n, width - n), F32)
    a_ref[:, :n] = 0.5 * (s + s.T)
    a_ref[...] += jnp.where(sub == lane, 1.0, 0.0)

    def step(t, _):
        first = t * PIVOTS
        a = a_ref[...]
        hits = [lane == first + b for b in range(PIVOTS)]
        rows = [a_ref[pl.ds(first + b, 1), :] for b in range(PIVOTS)]
        p = [[jnp.sum(jnp.where(h, r, 0.0), axis=1, keepdims=True) for h in hits] for r in rows]
        cols = [jnp.sum(jnp.where(h, a, 0.0), axis=1, keepdims=True) for h in hits]
        for i in range(PIVOTS):
            inv = 1.0 / p[i][i]
            scaled = [inv if j == i else p[i][j] * inv for j in range(PIVOTS)]
            for o in range(PIVOTS):
                if o != i:
                    f = p[o][i]
                    p[o] = [-f * inv if j == i else p[o][j] - f * scaled[j] for j in range(PIVOTS)]
            p[i] = scaled
        in_lanes = (lane >= first) & (lane < first + PIVOTS)
        in_rows = (sub >= first) & (sub < first + PIVOTS)
        rows = [jnp.where(in_lanes, jnp.where(h, 1.0, 0.0), r) for h, r in zip(hits, rows)]
        out = jnp.where(in_rows | in_lanes, 0.0, a)
        for i in range(PIVOTS):
            new = p[i][0] * rows[0]
            for j in range(1, PIVOTS):
                new = new + p[i][j] * rows[j]
            out = out - jnp.where(in_rows, jnp.where(sub == first + i, -1.0, 0.0), cols[i]) * new
        a_ref[...] = out
        return 0

    lax.fori_loop(0, n // PIVOTS, step, 0)
    o_ref[...] = a_ref[:, :n]


def inverse_of(inner, n):
    width = -(-n // LANES) * LANES
    return pl.pallas_call(
        inverse_kernel,
        out_shape=jax.ShapeDtypeStruct((n, n), F32),
        in_specs=[VMEM],
        out_specs=VMEM,
        scratch_shapes=[pltpu.VMEM((n, width), F32)],
        cost_estimate=pl.CostEstimate(flops=2 * n**3, bytes_accessed=8 * n * n, transcendentals=0),
        compiler_params=SMALL,
        name="inverse",
    )(inner)


def place_kernel(n, table, *refs):
    *piece_refs, high_ref, low_ref = refs
    for i, ref in enumerate(piece_refs):
        high_ref[table[i]], low_ref[table[i]] = halves(unpack(ref[...], n, high_ref.shape[2]))


def placed_halves(pieces, table, n, batch):
    shape = jax.ShapeDtypeStruct((len(pieces), n, batch), BF16)
    return pl.pallas_call(
        functools.partial(place_kernel, n),
        out_shape=(shape, shape),
        grid_spec=pltpu.PrefetchScalarGridSpec(
            num_scalar_prefetch=1, grid=(), in_specs=[VMEM] * len(pieces), out_specs=(VMEM, VMEM)
        ),
        compiler_params=SMALL,
        name="place",
    )(table, *pieces)


def product_kernel(a_ref, b_ref, o_ref):
    o_ref[...] = dot3(halves(a_ref[...]), halves(b_ref[...]), (1, 0))


def product_add_kernel(a_ref, b_ref, c_ref, o_ref):
    o_ref[...] = c_ref[...] + dot3(halves(a_ref[...]), halves(b_ref[...]), (1, 0))


def product(a, b, c=None):
    shape = a.shape[0], b.shape[1]
    return pl.pallas_call(
        product_kernel if c is None else product_add_kernel,
        out_shape=jax.ShapeDtypeStruct(shape, F32),
        in_specs=[VMEM] * (2 if c is None else 3),
        out_specs=VMEM,
        compiler_params=SMALL,
        name="product",
    )(*((a, b) if c is None else (a, b, c)))


def inner_kernel(n, batch, u_ref, x_ref, o_ref):
    inner = dot(unpack(u_ref[...], n, batch), unpack(x_ref[...], n, batch), (0, 0))
    for i in range(2):
        o_ref[i] = pack(inner[i * batch // 2 : (i + 1) * batch // 2])


def inner_of(u, x, n, batch):
    return pl.pallas_call(
        functools.partial(inner_kernel, n, batch),
        out_shape=jax.ShapeDtypeStruct((2, batch * batch // 2 // LANES, LANES), F32),
        in_specs=[VMEM] * 2,
        out_specs=VMEM,
        compiler_params=SMALL,
        name="inner",
    )(u, x)


def terms_kernel(n, streams, table, cov_ref, high_ref, low_ref, o_ref, *scratch):
    pieces, _, batch = high_ref.shape
    packed = n * batch // LANES
    count = o_ref.shape[0] // packed
    at = [pl.ds(pl.multiple_of(table[i] * n, 8), n) for i in range(count)]
    if streams:
        read_ref, sems = scratch
        copies = [pltpu.make_async_copy(cov_ref.at[at[i], :], read_ref.at[i], sems.at[i]) for i in range(count)]
        for copy in copies:
            copy.start()
    x = [ref[...].reshape(pieces * n, batch) for ref in (high_ref, low_ref)]
    for i in range(count):
        if streams:
            copies[i].wait()
        rows = read_ref[i] if streams else cov_ref[at[i], :]
        o_ref[i * packed : (i + 1) * packed, :] = pack(dot3(halves(rows), x, (1, 0)))


def row_terms(covariance, x_high, x_low, blocks, n, streams):
    width, batch = covariance.shape[1], x_high.shape[2]
    count = blocks.shape[0]
    return pl.pallas_call(
        functools.partial(terms_kernel, n, streams),
        out_shape=jax.ShapeDtypeStruct((count * n * batch // LANES, LANES), F32),
        grid_spec=pltpu.PrefetchScalarGridSpec(
            num_scalar_prefetch=1,
            grid=(),
            in_specs=[pl.BlockSpec(memory_space=pl.ANY) if streams else VMEM, VMEM, VMEM],
            out_specs=VMEM,
            scratch_shapes=[pltpu.VMEM((count, n, width), F32), pltpu.SemaphoreType.DMA((count,))] if streams else [],
        ),
        compiler_params=pltpu.CompilerParams(vmem_limit_bytes=46 * 2**20) if streams else SMALL,
        cost_estimate=pl.CostEstimate(
            flops=6 * count * n * width * batch, bytes_accessed=4 * count * n * width, transcendentals=0
        ),
        name="terms",
    )(blocks, covariance, x_high, x_low)


def gain_kernel(n, table, inverse_ref, *refs):
    *group_refs, high_ref, low_ref, own_ref, uh_ref, ul_ref = refs
    batch = inverse_ref.shape[0]
    size = n * batch // LANES
    per = group_refs[0].shape[0] // size
    count = len(group_refs) * per
    for i in range(count):
        packed = group_refs[i // per][i % per * size : (i % per + 1) * size, :]
        uh_ref[table[i]], ul_ref[table[i]] = halves(unpack(packed, n, batch))
    inverse = halves(inverse_ref[...])
    u = [ref[...].reshape(count * n, batch) for ref in (uh_ref, ul_ref)]
    high_ref[...], low_ref[...] = halves(dot3(inverse, u, (1, 1)))
    own_ref[...] = dot3((uh_ref[table[count]], ul_ref[table[count]]), inverse, (1, 0))


def gain_of(inverse, groups, table, n):
    batch = inverse.shape[0]
    count = table.shape[0] - 1
    shape = jax.ShapeDtypeStruct((batch, count * n), BF16)
    return pl.pallas_call(
        functools.partial(gain_kernel, n),
        out_shape=(shape, shape, jax.ShapeDtypeStruct((n, batch), F32)),
        grid_spec=pltpu.PrefetchScalarGridSpec(
            num_scalar_prefetch=1,
            grid=(),
            in_specs=[VMEM] * (1 + len(groups)),
            out_specs=(VMEM,) * 3,
            scratch_shapes=[pltpu.VMEM((count, n, batch), BF16)] * 2,
        ),
        compiler_params=SMALL,
        name="gain",
    )(table, inverse, *groups)


def update_kernel(n, table, cov_ref, high_ref, low_ref, *refs):
    *group_refs, o_ref, stage_ref, sems = refs
    batch = high_ref.shape[0]
    size = n * batch // LANES
    per = group_refs[0].shape[0] // size
    gain = high_ref[...], low_ref[...]
    copies = []
    for i in range(len(group_refs) * per):
        at = pl.ds(pl.multiple_of(table[i] * n, 8), n)
        rows = halves(unpack(group_refs[i // per][i % per * size : (i % per + 1) * size, :], n, batch))
        stage_ref[i] = cov_ref[at, :] - dot3(rows, gain, (1, 0))
        copies.append(pltpu.make_async_copy(stage_ref.at[i], o_ref.at[at, :], sems.at[i]))
        copies[i].start()
    for copy in copies:
        copy.wait()


def updated(covariance, gain_high, gain_low, groups, table, n):
    count, width = covariance.shape[0] // n, covariance.shape[1]
    return pl.pallas_call(
        functools.partial(update_kernel, n),
        out_shape=jax.ShapeDtypeStruct(covariance.shape, F32),
        grid_spec=pltpu.PrefetchScalarGridSpec(
            num_scalar_prefetch=1,
            grid=(),
            in_specs=[VMEM] * (3 + len(groups)),
            out_specs=pl.BlockSpec(memory_space=pl.ANY),
            scratch_shapes=[pltpu.VMEM((count, n, width), F32), pltpu.SemaphoreType.DMA((count,))],
        ),
        compiler_params=SMALL,
        name="update",
    )(table, covariance, gain_high, gain_low, *groups)


def program(nr, nc):
    k = nc // nr
    assert k == 2

    def swap(a, axis, mask):
        n = nr if axis == "row" else nc
        return lax.ppermute(a, axis, [(i, i ^ mask) for i in range(n)])

    def bits_of(n):
        return [1 << b for b in range(n.bit_length() - 1)]

    def on_device(covariance, samples, labels, weights):
        row, col = lax.axis_index("row"), lax.axis_index("col")
        z, x = col // k, col % k
        batch, piece = samples.shape
        fits = packs(piece, batch)

        def ordered(low, mine, other):
            return jnp.where(low, mine, other), jnp.where(low, other, mine)

        xt = pack(samples.T)
        size = xt.shape[0]
        x_by = {0: xt}
        for mask in reversed(bits_of(nr)):
            for d in list(x_by):
                x_by[d | mask] = swap(x_by[d], "row", mask)
        transposed = [
            (z_ * nc + k * r_ + x_, r_ * nc + k * z_ + x_) for r_ in range(nr) for z_ in range(nr) for x_ in range(k)
        ]
        x_piece = lax.ppermute(xt, ("row", "col"), transposed)
        offsets = jnp.arange(nr, dtype=jnp.int32)
        by_row = jnp.bitwise_xor(row, offsets)
        by_z = jnp.bitwise_xor(z, offsets)

        predicted = product(samples, weights) if fits else dot(samples, weights, (1, 0))
        steps = [("row", row, m) for m in bits_of(nr)] + [("col", col, m) for m in bits_of(k)]
        for axis, index, mask in steps:
            n = predicted.shape[0] // 2
            low = (index & mask) == 0
            a, b = predicted[:n], predicted[n:]
            predicted = jnp.where(low, a, b) + swap(jnp.where(low, b, a), axis, mask)
        for mask in bits_of(nr):
            predicted = predicted + swap(predicted, "col", mask * k)
        for axis, index, mask in reversed(steps):
            predicted = jnp.concatenate(ordered((index & mask) == 0, predicted, swap(predicted, axis, mask)))

        order = list(reversed(range(nr)))
        groups = [order[: nr // 2], order[nr // 2 :]]
        if fits:
            x_high, x_low = placed_halves([x_by[d] for d in range(nr)], by_row, piece, batch)

            def terms_of(e, group):
                blocks = jnp.bitwise_xor(x, e) * nr + jnp.bitwise_xor(z, jnp.array(group, jnp.int32))
                return row_terms(covariance, x_high, x_low, blocks, piece, e == 1 and group is groups[0])
        else:
            x_cols = jnp.concatenate([x_by[0]] * nr)
            for d in range(nr):
                x_cols = lax.dynamic_update_slice_in_dim(x_cols, x_by[d], by_row[d] * piece, 0)
            whole = dot(covariance, x_cols, (1, 0), HIGH)

            def terms_of(e, group):
                at = [(jnp.bitwise_xor(x, e) * nr + jnp.bitwise_xor(z, d)) * piece for d in group]
                return jnp.concatenate([lax.dynamic_slice_in_dim(whole, i, piece, 0) for i in at])

        sent = [swap(terms_of(1, group), "col", 1) for group in groups]
        part = {}
        for group, got in zip(groups, sent):
            kept = terms_of(0, group)
            for i, d in enumerate(group):
                part[d] = kept[i * size : (i + 1) * size] + got[i * size : (i + 1) * size]
        for mask in bits_of(nr):
            for d in sorted(part, reverse=True):
                if d & mask:
                    part[d ^ mask] = part[d ^ mask] + swap(part.pop(d), "col", mask * k)
        u_piece = part[0]

        if fits:
            inner = inner_of(u_piece, x_piece, piece, batch)
        else:
            inner = dot(u_piece, x_piece, (0, 0)).reshape(2, batch // 2, batch)
        low = (row & 1) == 0
        inner = jnp.where(low, inner[0], inner[1]) + swap(jnp.where(low, inner[1], inner[0]), "row", 1)
        for mask in bits_of(nr)[1:]:
            inner = inner + swap(inner, "row", mask)
        for mask in bits_of(nc):
            inner = inner + swap(inner, "col", mask)
        inner = jnp.stack(ordered(low, inner, swap(inner, "row", 1)))
        if not fits:
            inner = inner.reshape(batch, batch)

        u_by = {0: u_piece}
        for mask in reversed(bits_of(nr)):
            for d in list(u_by):
                u_by[d | mask] = swap(u_by[d], "col", mask * k)
        near = sorted(u_by)[: nr // 2]
        far = sorted(u_by)[nr // 2 :]
        own = [jnp.concatenate([u_by[d] for d in part_]) for part_ in (near, far)]
        peer = [swap(a, "col", 1) for a in own]
        u_cols = list(own)
        for mask in reversed(bits_of(nr)):
            pairs = [
                (r_ * nc + c_, (r_ ^ mask) * nc + c_)
                for c_ in range(nc)
                for r_ in range(nr)
                if (r_ ^ (c_ // k)) & (2 * mask - 1) == 0
            ]
            take = (jnp.bitwise_xor(row, z) & mask) != 0
            u_cols = [jnp.where(take, lax.ppermute(a, ("row", "col"), pairs), a) for a in u_cols]

        if fits:
            inverse = inverse_of(inner, batch)
            table = jnp.concatenate([by_z, row[None].astype(jnp.int32)])
            gain_high, gain_low, gain_piece = gain_of(inverse, u_cols, table, piece)
            table = jnp.concatenate([x * nr + by_z, (1 - x) * nr + by_z])
            new_covariance = updated(covariance, gain_high, gain_low, own + peer, table, piece)
        else:

            def in_order(pieces):
                out = jnp.concatenate(pieces)
                for a, group in zip(pieces, (near, far)):
                    for i, d in enumerate(group):
                        got = a[i * piece : (i + 1) * piece]
                        out = lax.dynamic_update_slice_in_dim(out, got, by_z[d] * piece, 0)
                return out

            inverse = inverse_of(inner, batch)
            gain = dot(in_order(u_cols), inverse, (1, 0))
            gain_piece = lax.dynamic_slice_in_dim(gain, row * piece, piece, 0)
            u_rows = jnp.concatenate(ordered(x == 0, in_order(own), in_order(peer)))
            new_covariance = covariance - dot(u_rows, gain, (1, 1), HIGH)
        classes = lax.broadcasted_iota(jnp.int32, (batch, weights.shape[1]), 1)
        targets = (labels[:, None] == classes).astype(F32)
        if fits:
            new_weights = product(gain_piece, targets - predicted, weights)
        else:
            new_weights = weights + dot(gain_piece, targets - predicted, (1, 0))
        return new_covariance, new_weights

    return on_device


def solution(mesh):
    return jax.shard_map(
        program(mesh.shape["row"], mesh.shape["col"]),
        mesh=mesh,
        in_specs=(P("row", "col"), P(None, ("col", "row")), P(), P(("col", "row"), None)),
        out_specs=(P("row", "col"), P(("col", "row"), None)),
        check_vma=False,
    )
```

```python
import functools

import jax
import jax.numpy as jnp
from jax import lax
from jax.experimental import pallas as pl
from jax.experimental.pallas import tpu as pltpu
from jax.sharding import PartitionSpec as P


HIGHEST = lax.Precision.HIGHEST
HIGH = lax.Precision.HIGH
F32, BF16 = jnp.float32, jnp.bfloat16
LANES = 128
PIVOTS = 4
SMALL = pltpu.CompilerParams(vmem_limit_bytes=20 * 2**20)
VMEM = pl.BlockSpec(memory_space=pltpu.VMEM)


def dot(a, b, dims, precision=HIGHEST):
    return lax.dot_general(a, b, ((dims[:1], dims[1:]), ((), ())), precision=precision, preferred_element_type=F32)


def halves(a):
    high = a.astype(BF16)
    return high, (a - high.astype(F32)).astype(BF16)


def dot3(a, b, dims):
    (ah, al), (bh, bl) = a, b
    return dot(ah, bh, dims, None) + (dot(ah, bl, dims, None) + dot(al, bh, dims, None))


def packs(n, batch):
    return batch == LANES * 3 // 2 and n % 16 == 0


def pack(a):
    n, batch = a.shape
    if not packs(n, batch):
        return a
    tail = a[:, LANES:]
    return jnp.concatenate([a[:, :LANES], jnp.concatenate([tail[: n // 2], tail[n // 2 :]], axis=1)])


def unpack(a, n, batch):
    if not packs(n, batch):
        return a
    tail = a[n:]
    side = LANES // 2
    return jnp.concatenate([a[:n], jnp.concatenate([tail[:, :side], tail[:, side:]])], axis=1)


def inverse_kernel(first, last, s_ref, o_ref):
    n, width = o_ref.shape
    lane = lax.broadcasted_iota(jnp.int32, (1, width), 1)
    sub = lax.broadcasted_iota(jnp.int32, (n, 1), 0)
    if first == 0:
        s = s_ref[...]
        if len(s.shape) == 3:
            s = jnp.concatenate([unpack(s_ref[i], n // 2, n) for i in range(2)])
        if width > n:
            o_ref[:, n:] = jnp.zeros((n, width - n), F32)
        o_ref[:, :n] = 0.5 * (s + s.T)
        o_ref[...] += jnp.where(sub == lane, 1.0, 0.0)
    else:
        o_ref[...] = s_ref[...]

    def step(t, _):
        at = t * PIVOTS
        a = o_ref[...]
        hits = [lane == at + b for b in range(PIVOTS)]
        rows = [o_ref[pl.ds(at + b, 1), :] for b in range(PIVOTS)]
        p = [[jnp.sum(jnp.where(h, r, 0.0), axis=1, keepdims=True) for h in hits] for r in rows]
        cols = [jnp.sum(jnp.where(h, a, 0.0), axis=1, keepdims=True) for h in hits]
        for i in range(PIVOTS):
            inv = 1.0 / p[i][i]
            scaled = [inv if j == i else p[i][j] * inv for j in range(PIVOTS)]
            for o in range(PIVOTS):
                if o != i:
                    f = p[o][i]
                    p[o] = [-f * inv if j == i else p[o][j] - f * scaled[j] for j in range(PIVOTS)]
            p[i] = scaled
        in_lanes = (lane >= at) & (lane < at + PIVOTS)
        in_rows = (sub >= at) & (sub < at + PIVOTS)
        rows = [jnp.where(in_lanes, jnp.where(h, 1.0, 0.0), r) for h, r in zip(hits, rows)]
        out = jnp.where(in_rows | in_lanes, 0.0, a)
        for i in range(PIVOTS):
            new = p[i][0] * rows[0]
            for j in range(1, PIVOTS):
                new = new + p[i][j] * rows[j]
            out = out - jnp.where(in_rows, jnp.where(sub == at + i, -1.0, 0.0), cols[i]) * new
        o_ref[...] = out
        return 0

    lax.fori_loop(first, last, step, 0)


def eliminated(a, n, first, last):
    width = -(-n // LANES) * LANES
    return pl.pallas_call(
        functools.partial(inverse_kernel, first, last),
        out_shape=jax.ShapeDtypeStruct((n, width), F32),
        in_specs=[VMEM],
        out_specs=VMEM,
        compiler_params=SMALL,
        cost_estimate=pl.CostEstimate(flops=2 * n**3, bytes_accessed=8 * n * n, transcendentals=0),
        name="inverse",
    )(a)


def place_kernel(n, place, *refs):
    *piece_refs, high_ref, low_ref = refs
    for i, ref in enumerate(piece_refs):
        at = place[0] ^ i
        high_ref[at], low_ref[at] = halves(unpack(ref[...], n, high_ref.shape[2]))


def placed_halves(pieces, place, n, batch):
    shape = jax.ShapeDtypeStruct((len(pieces), n, batch), BF16)
    return pl.pallas_call(
        functools.partial(place_kernel, n),
        out_shape=(shape, shape),
        grid_spec=pltpu.PrefetchScalarGridSpec(
            num_scalar_prefetch=1, grid=(), in_specs=[VMEM] * len(pieces), out_specs=(VMEM, VMEM)
        ),
        compiler_params=SMALL,
        name="place",
    )(place, *pieces)


def product_kernel(a_ref, b_ref, o_ref):
    o_ref[...] = dot3(halves(a_ref[...]), halves(b_ref[...]), (1, 0))


def product_add_kernel(a_ref, b_ref, c_ref, o_ref):
    o_ref[...] = c_ref[...] + dot3(halves(a_ref[...]), halves(b_ref[...]), (1, 0))


def product(a, b, c=None):
    shape = a.shape[0], b.shape[1]
    return pl.pallas_call(
        product_kernel if c is None else product_add_kernel,
        out_shape=jax.ShapeDtypeStruct(shape, F32),
        in_specs=[VMEM] * (2 if c is None else 3),
        out_specs=VMEM,
        compiler_params=SMALL,
        name="product",
    )(*((a, b) if c is None else (a, b, c)))


def inner_kernel(n, batch, *refs):
    *in_refs, o_ref = refs
    half = len(in_refs) // 2
    inner = 0.0
    for u_ref, x_ref in zip(in_refs[:half], in_refs[half:]):
        inner = inner + dot(unpack(u_ref[...], n, batch), unpack(x_ref[...], n, batch), (0, 0))
    for i in range(2):
        o_ref[i] = pack(inner[i * batch // 2 : (i + 1) * batch // 2])


def inner_of(u, x, n, batch):
    return pl.pallas_call(
        functools.partial(inner_kernel, n, batch),
        out_shape=jax.ShapeDtypeStruct((2, batch * batch // 2 // LANES, LANES), F32),
        in_specs=[VMEM] * (2 * len(u)),
        out_specs=VMEM,
        compiler_params=SMALL,
        name="inner",
    )(*u, *x)


def terms_kernel(n, streams, e, group, place, cov_ref, high_ref, low_ref, o_ref, *scratch):
    pieces, _, batch = high_ref.shape
    packed = n * batch // LANES
    count = o_ref.shape[0] // packed
    at = [pl.ds(pl.multiple_of(((place[2] ^ e) * pieces + (place[1] ^ d)) * n, 8), n) for d in group]
    if streams:
        read_ref, sems = scratch
        copies = [pltpu.make_async_copy(cov_ref.at[at[i], :], read_ref.at[i], sems.at[i]) for i in range(count)]
        for copy in copies:
            copy.start()
    x = [ref[...].reshape(pieces * n, batch) for ref in (high_ref, low_ref)]
    for i in range(count):
        if streams:
            copies[i].wait()
        rows = read_ref[i] if streams else cov_ref[at[i], :]
        o_ref[i * packed : (i + 1) * packed, :] = pack(dot3(halves(rows), x, (1, 0)))


def row_terms(covariance, x_high, x_low, place, e, group, n, streams):
    width, batch = covariance.shape[1], x_high.shape[2]
    count = len(group)
    return pl.pallas_call(
        functools.partial(terms_kernel, n, streams, e, tuple(group)),
        out_shape=jax.ShapeDtypeStruct((count * n * batch // LANES, LANES), F32),
        grid_spec=pltpu.PrefetchScalarGridSpec(
            num_scalar_prefetch=1,
            grid=(),
            in_specs=[pl.BlockSpec(memory_space=pl.ANY) if streams else VMEM, VMEM, VMEM],
            out_specs=VMEM,
            scratch_shapes=[pltpu.VMEM((count, n, width), F32), pltpu.SemaphoreType.DMA((count,))] if streams else [],
        ),
        compiler_params=pltpu.CompilerParams(vmem_limit_bytes=46 * 2**20) if streams else SMALL,
        cost_estimate=pl.CostEstimate(
            flops=6 * count * n * width * batch, bytes_accessed=4 * count * n * width, transcendentals=0
        ),
        name="terms",
    )(place, covariance, x_high, x_low)


def gain_kernel(n, place, inverse_ref, *refs):
    *group_refs, high_ref, low_ref, own_ref, uh_ref, ul_ref = refs
    batch = inverse_ref.shape[0]
    size = n * batch // LANES
    per = group_refs[0].shape[0] // size
    count = len(group_refs) * per
    for i in range(count):
        packed = group_refs[i // per][i % per * size : (i % per + 1) * size, :]
        at = place[1] ^ i
        uh_ref[at], ul_ref[at] = halves(unpack(packed, n, batch))
    inverse = halves(inverse_ref[:, :batch])
    u = [ref[...].reshape(count * n, batch) for ref in (uh_ref, ul_ref)]
    high_ref[...], low_ref[...] = halves(dot3(inverse, u, (1, 1)))
    own_ref[...] = dot3((uh_ref[place[0]], ul_ref[place[0]]), inverse, (1, 0))


def gain_of(inverse, groups, place, n):
    batch = inverse.shape[0]
    count = sum(a.shape[0] for a in groups) // (n * batch // LANES)
    shape = jax.ShapeDtypeStruct((batch, count * n), BF16)
    return pl.pallas_call(
        functools.partial(gain_kernel, n),
        out_shape=(shape, shape, jax.ShapeDtypeStruct((n, batch), F32)),
        grid_spec=pltpu.PrefetchScalarGridSpec(
            num_scalar_prefetch=1,
            grid=(),
            in_specs=[VMEM] * (1 + len(groups)),
            out_specs=(VMEM,) * 3,
            scratch_shapes=[pltpu.VMEM((count, n, batch), BF16)] * 2,
        ),
        compiler_params=SMALL,
        name="gain",
    )(place, inverse, *groups)


def update_kernel(n, place, cov_ref, high_ref, low_ref, *refs):
    *group_refs, o_ref, stage_ref, sems = refs
    batch = high_ref.shape[0]
    size = n * batch // LANES
    per = group_refs[0].shape[0] // size
    pieces = high_ref.shape[1] // n
    gain = high_ref[...], low_ref[...]
    copies = []
    for i in range(len(group_refs) * per):
        block = (place[2] ^ (i // pieces)) * pieces + (place[1] ^ (i % pieces))
        at = pl.ds(pl.multiple_of(block * n, 8), n)
        rows = halves(unpack(group_refs[i // per][i % per * size : (i % per + 1) * size, :], n, batch))
        stage_ref[i] = cov_ref[at, :] - dot3(rows, gain, (1, 0))
        copies.append(pltpu.make_async_copy(stage_ref.at[i], o_ref.at[at, :], sems.at[i]))
        copies[i].start()
    for copy in copies:
        copy.wait()


def updated(covariance, gain_high, gain_low, groups, place, n):
    count, width = covariance.shape[0] // n, covariance.shape[1]
    return pl.pallas_call(
        functools.partial(update_kernel, n),
        out_shape=jax.ShapeDtypeStruct(covariance.shape, F32),
        grid_spec=pltpu.PrefetchScalarGridSpec(
            num_scalar_prefetch=1,
            grid=(),
            in_specs=[VMEM] * (3 + len(groups)),
            out_specs=pl.BlockSpec(memory_space=pl.ANY),
            scratch_shapes=[pltpu.VMEM((count, n, width), F32), pltpu.SemaphoreType.DMA((count,))],
        ),
        compiler_params=SMALL,
        name="update",
    )(place, covariance, gain_high, gain_low, *groups)


def after(a, *others):
    return lax.optimization_barrier((a, *others))[0]


def program(nr, nc):
    k = nc // nr
    assert k == 2

    def swap(a, axis, mask):
        n = nr if axis == "row" else nc
        return lax.ppermute(a, axis, [(i, i ^ mask) for i in range(n)])

    def bits_of(n):
        return [1 << b for b in range(n.bit_length() - 1)]

    masks = bits_of(nr)

    def on_device(covariance, samples, labels, weights):
        row, col = lax.axis_index("row"), lax.axis_index("col")
        z, x = lax.div(col, k), lax.rem(col, k)
        place = jnp.stack([row, z, x]).astype(jnp.int32)
        batch, piece = samples.shape
        fits = packs(piece, batch)

        first_of = {m: (row & m) == 0 for m in masks}
        handed_to = {m: ((row ^ z) & m) != 0 for m in masks}

        def ordered(low, mine, other):
            return jnp.where(low, mine, other), jnp.where(low, other, mine)

        xt = pack(samples.T)
        size = xt.shape[0]
        x_by = {0: xt}
        for mask in reversed(masks):
            for d in list(x_by):
                x_by[d | mask] = swap(x_by[d], "row", mask)
        order = list(reversed(range(nr)))
        groups = [order[: nr // 2], order[nr // 2 :]]

        if fits:
            x_high, x_low = placed_halves([x_by[d] for d in range(nr)], place, piece, batch)
            placed = x_high

            def terms_of(e, group, x_high):
                return row_terms(covariance, x_high, x_low, place, e, group, piece, e == 1 and group is groups[0])
        else:
            placed = jnp.concatenate([x_by[0]] * nr)
            for d in range(nr):
                placed = lax.dynamic_update_slice_in_dim(placed, x_by[d], (row ^ d) * piece, 0)
            whole = dot(covariance, placed, (1, 0), HIGH)

            def terms_of(e, group, _):
                at = [((x ^ e) * nr + (z ^ d)) * piece for d in group]
                return jnp.concatenate([lax.dynamic_slice_in_dim(whole, i, piece, 0) for i in at])

        predicted = product(samples, weights) if fits else dot(samples, weights, (1, 0))
        sends = [("row", row, m, True) for m in masks] + [("col", z, m * k, False) for m in masks]
        sends += [("col", x, 1, False)]

        def step_on(predicted, *others):
            axis, index, mask, halves_it = sends.pop(0)
            if halves_it:
                n = predicted.shape[0] // 2
                low = (index & mask) == 0
                a, b = predicted[:n], predicted[n:]
                keep, give = jnp.where(low, a, b), jnp.where(low, b, a)
            else:
                keep = give = predicted
            got = swap(give, axis, mask)
            predicted = keep + got
            return tuple(lax.optimization_barrier((predicted, *others)))

        transposed = [
            (z_ * nc + k * r_ + x_, r_ * nc + k * z_ + x_) for r_ in range(nr) for z_ in range(nr) for x_ in range(k)
        ]
        made, kept = [], []
        predicted, placed, first_of, handed_to = lax.optimization_barrier((predicted, placed, first_of, handed_to))
        made.append(terms_of(1, groups[0], placed))
        predicted, placed = step_on(predicted, placed)
        predicted = after(predicted, made[0])
        x_piece = lax.ppermute(after(xt, made[0]), ("row", "col"), transposed)
        made.append(terms_of(1, groups[1], placed))
        predicted, placed = step_on(predicted, placed)
        predicted = after(predicted, made[1])
        kept.append(terms_of(0, groups[0], placed))
        predicted, placed, x_piece = step_on(predicted, placed, x_piece)
        predicted = after(predicted, kept[0])
        kept.append(terms_of(0, groups[1], placed))
        sent = []
        for a in made:
            sent.append(swap(a, "col", 1))
        while len(sends) > 1:
            predicted, sent[0], kept[1] = step_on(predicted, sent[0], kept[1])
        x_far = swap(after(x_piece, kept[1]), "col", masks[-1] * k)
        predicted, sent[1] = lax.optimization_barrier((predicted, sent[1]))

        part = {}
        for group, a, b in zip(groups, kept, sent):
            for i, d in enumerate(group):
                part[d] = a[i * size : (i + 1) * size] + b[i * size : (i + 1) * size]
        for mask in masks[:-1]:
            for d in sorted(part, reverse=True):
                if d & mask:
                    got = swap(part.pop(d), "col", mask * k)
                    part[d ^ mask] = part[d ^ mask] + got
        last = masks[-1]
        predicted, part[0] = step_on(predicted, part[0])
        got = swap(part[last], "col", last * k)

        if fits:
            inner = inner_of([part[0], part[last]], [x_piece, x_far], piece, batch)
        else:
            inner = (dot(part[0], x_piece, (0, 0)) + dot(part[last], x_far, (0, 0))).reshape(2, batch // 2, batch)
        low = first_of[1]
        inner = jnp.where(low, inner[0], inner[1]) + swap(jnp.where(low, inner[1], inner[0]), "row", 1)
        for mask in masks[1:]:
            inner = inner + swap(inner, "row", mask)
        for mask in bits_of(k):
            hop = swap(inner, "col", mask)
            inner = inner + hop
        u_piece = part[0] + got
        for mask in reversed(masks):
            predicted = jnp.concatenate(ordered(first_of[mask], predicted, swap(predicted, "row", mask)))
            if mask > 1:
                predicted, u_piece = lax.optimization_barrier((predicted, u_piece))
        for mask in masks:
            inner = inner + swap(inner, "col", mask * k)
        inner = jnp.stack(ordered(low, inner, swap(inner, "row", 1)))
        if not fits:
            inner = inner.reshape(batch, batch)

        u_by = {0: u_piece}
        for d in range(1, nr):
            u_by[d] = swap(u_piece, "col", d * k)
        own = [jnp.concatenate([u_by[d] for d in range(nr // 2)])]
        peer = [swap(own[0], "col", 1)]

        def handed(a, mask):
            pairs = [
                (r_ * nc + c_, (r_ ^ mask) * nc + c_)
                for c_ in range(nc)
                for r_ in range(nr)
                if (r_ ^ (c_ // k)) & (2 * mask - 1) == 0
            ]
            return jnp.where(handed_to[mask], lax.ppermute(a, ("row", "col"), pairs), a)

        steps = batch // PIVOTS
        near = own[0]
        for mask in reversed(masks[1:]):
            near = handed(near, mask)
        inverse = eliminated(inner, batch, 0, steps // 3)
        inverse, near = lax.optimization_barrier((inverse, near))
        near = handed(near, 1)
        inverse = eliminated(inverse, batch, steps // 3, 2 * steps // 3)
        inverse, *far = lax.optimization_barrier((inverse, *(u_by[d] for d in range(nr // 2, nr))))
        own.append(jnp.concatenate(far))
        peer.append(swap(own[1], "col", 1))
        far = own[1]
        for mask in reversed(masks):
            far = handed(far, mask)
        inverse = eliminated(inverse, batch, 2 * steps // 3, steps)
        u_cols = [near, far]

        classes = lax.broadcasted_iota(jnp.int32, (batch, weights.shape[1]), 1)
        missed = (labels[:, None] == classes).astype(F32) - predicted
        if fits:
            gain_high, gain_low, gain_piece = gain_of(inverse, u_cols, place, piece)
            new_covariance = updated(covariance, gain_high, gain_low, own + peer, place, piece)
            new_weights = product(gain_piece, missed, weights)
        else:

            def in_order(pieces):
                joined = jnp.concatenate(pieces)
                out = joined
                for d in range(nr):
                    got = joined[d * piece : (d + 1) * piece]
                    out = lax.dynamic_update_slice_in_dim(out, got, (z ^ d) * piece, 0)
                return out

            gain = dot(in_order(u_cols), inverse[:, :batch], (1, 0))
            gain_piece = lax.dynamic_slice_in_dim(gain, row * piece, piece, 0)
            u_rows = jnp.concatenate(ordered(x == 0, in_order(own), in_order(peer)))
            new_covariance = covariance - dot(u_rows, gain, (1, 1), HIGH)
            new_weights = weights + dot(gain_piece, missed, (1, 0))
        return new_covariance, new_weights

    return on_device


def solution(mesh):
    on_device = program(mesh.shape["row"], mesh.shape["col"])

    return jax.shard_map(
        on_device,
        mesh=mesh,
        in_specs=(P("row", "col"), P(None, ("col", "row")), P(), P(("col", "row"), None)),
        out_specs=(P("row", "col"), P(("col", "row"), None)),
        check_vma=False,
    )
```

```python
import functools

import jax
import jax.numpy as jnp
from jax import lax
from jax.experimental import pallas as pl
from jax.experimental.pallas import tpu as pltpu
from jax.sharding import PartitionSpec as P


HIGHEST = lax.Precision.HIGHEST
HIGH = lax.Precision.HIGH
F32, BF16 = jnp.float32, jnp.bfloat16
LANES = 128
PIVOTS = 4
SMALL = pltpu.CompilerParams(vmem_limit_bytes=20 * 2**20)
VMEM = pl.BlockSpec(memory_space=pltpu.VMEM)


def dot(a, b, dims, precision=HIGHEST):
    return lax.dot_general(a, b, ((dims[:1], dims[1:]), ((), ())), precision=precision, preferred_element_type=F32)


def halves(a):
    high = a.astype(BF16)
    return high, (a - high.astype(F32)).astype(BF16)


def dot3(a, b, dims):
    (ah, al), (bh, bl) = a, b
    return dot(ah, bh, dims, None) + (dot(ah, bl, dims, None) + dot(al, bh, dims, None))


def packs(n, batch):
    return batch == LANES * 3 // 2 and n % 16 == 0


def pack(a):
    n, batch = a.shape
    if not packs(n, batch):
        return a
    tail = a[:, LANES:]
    return jnp.concatenate([a[:, :LANES], jnp.concatenate([tail[: n // 2], tail[n // 2 :]], axis=1)])


def unpack(a, n, batch):
    if not packs(n, batch):
        return a
    tail = a[n:]
    side = LANES // 2
    return jnp.concatenate([a[:n], jnp.concatenate([tail[:, :side], tail[:, side:]])], axis=1)


def inverse_kernel(first, last, s_ref, o_ref):
    n, width = o_ref.shape
    lane = lax.broadcasted_iota(jnp.int32, (1, width), 1)
    sub = lax.broadcasted_iota(jnp.int32, (n, 1), 0)
    if first == 0:
        s = s_ref[...]
        if len(s.shape) == 3:
            s = jnp.concatenate([unpack(s_ref[i], n // 2, n) for i in range(2)])
        if width > n:
            o_ref[:, n:] = jnp.zeros((n, width - n), F32)
        o_ref[:, :n] = 0.5 * (s + s.T)
        o_ref[...] += jnp.where(sub == lane, 1.0, 0.0)
    else:
        o_ref[...] = s_ref[...]

    def step(t, _):
        at = t * PIVOTS
        a = o_ref[...]
        hits = [lane == at + b for b in range(PIVOTS)]
        rows = [o_ref[pl.ds(at + b, 1), :] for b in range(PIVOTS)]
        p = [[jnp.sum(jnp.where(h, r, 0.0), axis=1, keepdims=True) for h in hits] for r in rows]
        cols = [jnp.sum(jnp.where(h, a, 0.0), axis=1, keepdims=True) for h in hits]
        for i in range(PIVOTS):
            inv = 1.0 / p[i][i]
            scaled = [inv if j == i else p[i][j] * inv for j in range(PIVOTS)]
            for o in range(PIVOTS):
                if o != i:
                    f = p[o][i]
                    p[o] = [-f * inv if j == i else p[o][j] - f * scaled[j] for j in range(PIVOTS)]
            p[i] = scaled
        in_lanes = (lane >= at) & (lane < at + PIVOTS)
        in_rows = (sub >= at) & (sub < at + PIVOTS)
        rows = [jnp.where(in_lanes, jnp.where(h, 1.0, 0.0), r) for h, r in zip(hits, rows)]
        out = jnp.where(in_rows | in_lanes, 0.0, a)
        for i in range(PIVOTS):
            new = p[i][0] * rows[0]
            for j in range(1, PIVOTS):
                new = new + p[i][j] * rows[j]
            out = out - jnp.where(in_rows, jnp.where(sub == at + i, -1.0, 0.0), cols[i]) * new
        o_ref[...] = out
        return 0

    lax.fori_loop(first, last, step, 0)


def eliminated(a, n, first, last):
    width = -(-n // LANES) * LANES
    return pl.pallas_call(
        functools.partial(inverse_kernel, first, last),
        out_shape=jax.ShapeDtypeStruct((n, width), F32),
        in_specs=[VMEM],
        out_specs=VMEM,
        compiler_params=SMALL,
        cost_estimate=pl.CostEstimate(flops=2 * n**3, bytes_accessed=8 * n * n, transcendentals=0),
        name="inverse",
    )(a)


def place_kernel(n, place, *refs):
    *piece_refs, high_ref, low_ref = refs
    for i, ref in enumerate(piece_refs):
        at = place[0] ^ i
        high_ref[at], low_ref[at] = halves(unpack(ref[...], n, high_ref.shape[2]))


def placed_halves(pieces, place, n, batch):
    shape = jax.ShapeDtypeStruct((len(pieces), n, batch), BF16)
    return pl.pallas_call(
        functools.partial(place_kernel, n),
        out_shape=(shape, shape),
        grid_spec=pltpu.PrefetchScalarGridSpec(
            num_scalar_prefetch=1, grid=(), in_specs=[VMEM] * len(pieces), out_specs=(VMEM, VMEM)
        ),
        compiler_params=SMALL,
        name="place",
    )(place, *pieces)


def product_kernel(a_ref, b_ref, o_ref):
    o_ref[...] = dot3(halves(a_ref[...]), halves(b_ref[...]), (1, 0))


def product_add_kernel(a_ref, b_ref, c_ref, o_ref):
    o_ref[...] = c_ref[...] + dot3(halves(a_ref[...]), halves(b_ref[...]), (1, 0))


def product(a, b, c=None):
    shape = a.shape[0], b.shape[1]
    return pl.pallas_call(
        product_kernel if c is None else product_add_kernel,
        out_shape=jax.ShapeDtypeStruct(shape, F32),
        in_specs=[VMEM] * (2 if c is None else 3),
        out_specs=VMEM,
        compiler_params=SMALL,
        name="product",
    )(*((a, b) if c is None else (a, b, c)))


def inner_kernel(n, batch, *refs):
    *in_refs, o_ref = refs
    half = len(in_refs) // 2
    inner = 0.0
    for u_ref, x_ref in zip(in_refs[:half], in_refs[half:]):
        inner = inner + dot(unpack(u_ref[...], n, batch), unpack(x_ref[...], n, batch), (0, 0))
    for i in range(2):
        o_ref[i] = pack(inner[i * batch // 2 : (i + 1) * batch // 2])


def inner_of(u, x, n, batch):
    return pl.pallas_call(
        functools.partial(inner_kernel, n, batch),
        out_shape=jax.ShapeDtypeStruct((2, batch * batch // 2 // LANES, LANES), F32),
        in_specs=[VMEM] * (2 * len(u)),
        out_specs=VMEM,
        compiler_params=SMALL,
        name="inner",
    )(*u, *x)


def terms_kernel(n, streams, e, group, place, cov_ref, high_ref, low_ref, o_ref, *scratch):
    pieces, _, batch = high_ref.shape
    packed = n * batch // LANES
    count = o_ref.shape[0] // packed
    at = [pl.ds(pl.multiple_of(((place[2] ^ e) * pieces + (place[1] ^ d)) * n, 8), n) for d in group]
    if streams:
        read_ref, sems = scratch
        copies = [pltpu.make_async_copy(cov_ref.at[at[i], :], read_ref.at[i], sems.at[i]) for i in range(count)]
        for copy in copies:
            copy.start()
    x = [ref[...].reshape(pieces * n, batch) for ref in (high_ref, low_ref)]
    for i in range(count):
        if streams:
            copies[i].wait()
        rows = read_ref[i] if streams else cov_ref[at[i], :]
        o_ref[i * packed : (i + 1) * packed, :] = pack(dot3(halves(rows), x, (1, 0)))


def row_terms(covariance, x_high, x_low, place, e, group, n, streams):
    width, batch = covariance.shape[1], x_high.shape[2]
    count = len(group)
    return pl.pallas_call(
        functools.partial(terms_kernel, n, streams, e, tuple(group)),
        out_shape=jax.ShapeDtypeStruct((count * n * batch // LANES, LANES), F32),
        grid_spec=pltpu.PrefetchScalarGridSpec(
            num_scalar_prefetch=1,
            grid=(),
            in_specs=[pl.BlockSpec(memory_space=pl.ANY) if streams else VMEM, VMEM, VMEM],
            out_specs=VMEM,
            scratch_shapes=[pltpu.VMEM((count, n, width), F32), pltpu.SemaphoreType.DMA((count,))] if streams else [],
        ),
        compiler_params=pltpu.CompilerParams(vmem_limit_bytes=46 * 2**20) if streams else SMALL,
        cost_estimate=pl.CostEstimate(
            flops=6 * count * n * width * batch, bytes_accessed=4 * count * n * width, transcendentals=0
        ),
        name="terms",
    )(place, covariance, x_high, x_low)


def gain_kernel(n, place, inverse_ref, *refs):
    *group_refs, high_ref, low_ref, own_ref, uh_ref, ul_ref = refs
    batch = inverse_ref.shape[0]
    size = n * batch // LANES
    per = group_refs[0].shape[0] // size
    count = len(group_refs) * per
    for i in range(count):
        packed = group_refs[i // per][i % per * size : (i % per + 1) * size, :]
        at = place[1] ^ i
        uh_ref[at], ul_ref[at] = halves(unpack(packed, n, batch))
    inverse = halves(inverse_ref[:, :batch])
    u = [ref[...].reshape(count * n, batch) for ref in (uh_ref, ul_ref)]
    high_ref[...], low_ref[...] = halves(dot3(inverse, u, (1, 1)))
    own_ref[...] = dot3((uh_ref[place[0]], ul_ref[place[0]]), inverse, (1, 0))


def gain_of(inverse, groups, place, n):
    batch = inverse.shape[0]
    count = sum(a.shape[0] for a in groups) // (n * batch // LANES)
    shape = jax.ShapeDtypeStruct((batch, count * n), BF16)
    return pl.pallas_call(
        functools.partial(gain_kernel, n),
        out_shape=(shape, shape, jax.ShapeDtypeStruct((n, batch), F32)),
        grid_spec=pltpu.PrefetchScalarGridSpec(
            num_scalar_prefetch=1,
            grid=(),
            in_specs=[VMEM] * (1 + len(groups)),
            out_specs=(VMEM,) * 3,
            scratch_shapes=[pltpu.VMEM((count, n, batch), BF16)] * 2,
        ),
        compiler_params=SMALL,
        name="gain",
    )(place, inverse, *groups)


def update_kernel(n, place, cov_ref, high_ref, low_ref, *refs):
    *group_refs, o_ref, stage_ref, sems = refs
    batch = high_ref.shape[0]
    size = n * batch // LANES
    per = group_refs[0].shape[0] // size
    pieces = high_ref.shape[1] // n
    gain = high_ref[...], low_ref[...]
    copies = []
    for i in range(len(group_refs) * per):
        block = (place[2] ^ (i // pieces)) * pieces + (place[1] ^ (i % pieces))
        at = pl.ds(pl.multiple_of(block * n, 8), n)
        rows = halves(unpack(group_refs[i // per][i % per * size : (i % per + 1) * size, :], n, batch))
        stage_ref[i] = cov_ref[at, :] - dot3(rows, gain, (1, 0))
        copies.append(pltpu.make_async_copy(stage_ref.at[i], o_ref.at[at, :], sems.at[i]))
        copies[i].start()
    for copy in copies:
        copy.wait()


def updated(covariance, gain_high, gain_low, groups, place, n):
    count, width = covariance.shape[0] // n, covariance.shape[1]
    return pl.pallas_call(
        functools.partial(update_kernel, n),
        out_shape=jax.ShapeDtypeStruct(covariance.shape, F32),
        grid_spec=pltpu.PrefetchScalarGridSpec(
            num_scalar_prefetch=1,
            grid=(),
            in_specs=[VMEM] * (3 + len(groups)),
            out_specs=pl.BlockSpec(memory_space=pl.ANY),
            scratch_shapes=[pltpu.VMEM((count, n, width), F32), pltpu.SemaphoreType.DMA((count,))],
        ),
        compiler_params=SMALL,
        name="update",
    )(place, covariance, gain_high, gain_low, *groups)


def after(a, *others):
    return lax.optimization_barrier((a, *others))[0]


def program(nr, nc):
    k = nc // nr
    assert k == 2

    def swap(a, axis, mask):
        n = nr if axis == "row" else nc
        return lax.ppermute(a, axis, [(i, i ^ mask) for i in range(n)])

    def bits_of(n):
        return [1 << b for b in range(n.bit_length() - 1)]

    masks = bits_of(nr)

    def on_device(covariance, samples, labels, weights):
        row, col = lax.axis_index("row"), lax.axis_index("col")
        z, x = lax.div(col, k), lax.rem(col, k)
        place = jnp.stack([row, z, x]).astype(jnp.int32)
        batch, piece = samples.shape
        fits = packs(piece, batch)

        first_of = {m: (row & m) == 0 for m in masks}
        handed_to = {m: ((row ^ z) & m) != 0 for m in masks}

        def ordered(low, mine, other):
            return jnp.where(low, mine, other), jnp.where(low, other, mine)

        xt = pack(samples.T)
        size = xt.shape[0]
        x_by = {0: xt}
        for mask in reversed(masks):
            for d in list(x_by):
                x_by[d | mask] = swap(x_by[d], "row", mask)
        order = list(reversed(range(nr)))
        groups = [order[: nr // 2], order[nr // 2 :]]

        if fits:
            x_high, x_low = placed_halves([x_by[d] for d in range(nr)], place, piece, batch)
            placed = x_high

            def terms_of(e, group, x_high):
                return row_terms(covariance, x_high, x_low, place, e, group, piece, e == 1 and group is groups[0])
        else:
            placed = jnp.concatenate([x_by[0]] * nr)
            for d in range(nr):
                placed = lax.dynamic_update_slice_in_dim(placed, x_by[d], (row ^ d) * piece, 0)
            whole = dot(covariance, placed, (1, 0), HIGH)

            def terms_of(e, group, _):
                at = [((x ^ e) * nr + (z ^ d)) * piece for d in group]
                return jnp.concatenate([lax.dynamic_slice_in_dim(whole, i, piece, 0) for i in at])

        predicted = product(samples, weights) if fits else dot(samples, weights, (1, 0))
        sends = [("row", row, m, True) for m in masks] + [("col", z, m * k, False) for m in masks]
        sends += [("col", x, 1, False)]

        def step_on(predicted, *others):
            axis, index, mask, halves_it = sends.pop(0)
            if halves_it:
                n = predicted.shape[0] // 2
                low = (index & mask) == 0
                a, b = predicted[:n], predicted[n:]
                keep, give = jnp.where(low, a, b), jnp.where(low, b, a)
            else:
                keep = give = predicted
            got = swap(give, axis, mask)
            predicted = keep + got
            return tuple(lax.optimization_barrier((predicted, *others)))

        transposed = [
            (z_ * nc + k * r_ + x_, r_ * nc + k * z_ + x_) for r_ in range(nr) for z_ in range(nr) for x_ in range(k)
        ]
        x_piece = lax.ppermute(xt, ("row", "col"), transposed)
        predicted, placed = step_on(predicted, placed)
        placed, first_of, handed_to = lax.optimization_barrier((placed, first_of, handed_to))
        made = [terms_of(1, group, placed) for group in groups]
        sent = []
        for a in made:
            sent.append(swap(a, "col", 1))
        kept = [terms_of(0, group, placed) for group in groups]
        predicted = after(predicted, made[0])
        while sends[0][0] == "row":
            (predicted,) = step_on(predicted)
        predicted, kept[1], x_piece = lax.optimization_barrier((predicted, kept[1], x_piece))
        while len(sends) > 2:
            (predicted,) = step_on(predicted)
        predicted, sent[0] = lax.optimization_barrier((predicted, sent[0]))

        part = {}
        for group, a, b in zip(groups, kept, sent):
            for i, d in enumerate(group):
                part[d] = a[i * size : (i + 1) * size] + b[i * size : (i + 1) * size]
        for mask in masks:
            for d in sorted(part, reverse=True):
                if d & mask:
                    got = swap(part.pop(d), "col", mask * k)
                    part[d ^ mask] = part[d ^ mask] + got
        while len(sends) > 1:
            (predicted,) = step_on(predicted)
        (predicted,) = step_on(predicted)
        predicted, u_piece = lax.optimization_barrier((predicted, part[0]))

        if fits:
            inner = inner_of([u_piece], [x_piece], piece, batch)
        else:
            inner = dot(u_piece, x_piece, (0, 0)).reshape(2, batch // 2, batch)
        low = first_of[1]
        inner = jnp.where(low, inner[0], inner[1]) + swap(jnp.where(low, inner[1], inner[0]), "row", 1)
        for mask in masks[1:]:
            inner = inner + swap(inner, "row", mask)
        for mask in bits_of(k):
            hop = swap(inner, "col", mask)
            inner = inner + hop
        for mask in masks:
            inner = inner + swap(inner, "col", mask * k)
        inner = jnp.stack(ordered(low, inner, swap(inner, "row", 1)))
        if not fits:
            inner = inner.reshape(batch, batch)
        for mask in reversed(masks):
            got = swap(predicted, "row", mask)
            predicted = jnp.concatenate(ordered(first_of[mask], predicted, got))

        u_by = {0: u_piece}
        for d in range(1, nr):
            u_by[d] = swap(u_piece, "col", d * k)
        own = [jnp.concatenate([u_by[d] for d in range(nr // 2)])]
        peer = [swap(own[0], "col", 1)]

        def handed(a, mask):
            pairs = [
                (r_ * nc + c_, (r_ ^ mask) * nc + c_)
                for c_ in range(nc)
                for r_ in range(nr)
                if (r_ ^ (c_ // k)) & (2 * mask - 1) == 0
            ]
            return jnp.where(handed_to[mask], lax.ppermute(a, ("row", "col"), pairs), a)

        steps = batch // PIVOTS
        near = own[0]
        for mask in reversed(masks[1:]):
            near = handed(near, mask)
        inverse = eliminated(inner, batch, 0, steps // 3)
        inverse, near = lax.optimization_barrier((inverse, near))
        near = handed(near, 1)
        inverse = eliminated(inverse, batch, steps // 3, 2 * steps // 3)
        inverse, *far = lax.optimization_barrier((inverse, *(u_by[d] for d in range(nr // 2, nr))))
        own.append(jnp.concatenate(far))
        peer.append(swap(own[1], "col", 1))
        far = own[1]
        for mask in reversed(masks):
            far = handed(far, mask)
        inverse = eliminated(inverse, batch, 2 * steps // 3, steps)
        u_cols = [near, far]

        classes = lax.broadcasted_iota(jnp.int32, (batch, weights.shape[1]), 1)
        missed = (labels[:, None] == classes).astype(F32) - predicted
        if fits:
            gain_high, gain_low, gain_piece = gain_of(inverse, u_cols, place, piece)
            new_covariance = updated(covariance, gain_high, gain_low, own + peer, place, piece)
            new_weights = product(gain_piece, missed, weights)
        else:

            def in_order(pieces):
                joined = jnp.concatenate(pieces)
                out = joined
                for d in range(nr):
                    got = joined[d * piece : (d + 1) * piece]
                    out = lax.dynamic_update_slice_in_dim(out, got, (z ^ d) * piece, 0)
                return out

            gain = dot(in_order(u_cols), inverse[:, :batch], (1, 0))
            gain_piece = lax.dynamic_slice_in_dim(gain, row * piece, piece, 0)
            u_rows = jnp.concatenate(ordered(x == 0, in_order(own), in_order(peer)))
            new_covariance = covariance - dot(u_rows, gain, (1, 1), HIGH)
            new_weights = weights + dot(gain_piece, missed, (1, 0))
        return new_covariance, new_weights

    return on_device


def solution(mesh):
    on_device = program(mesh.shape["row"], mesh.shape["col"])

    return jax.shard_map(
        on_device,
        mesh=mesh,
        in_specs=(P("row", "col"), P(None, ("col", "row")), P(), P(("col", "row"), None)),
        out_specs=(P("row", "col"), P(("col", "row"), None)),
        check_vma=False,
    )
```

```python
import functools

import jax
import jax.numpy as jnp
from jax import lax
from jax.experimental import pallas as pl
from jax.experimental.pallas import tpu as pltpu
from jax.sharding import PartitionSpec as P


HIGHEST = lax.Precision.HIGHEST
HIGH = lax.Precision.HIGH
F32, BF16 = jnp.float32, jnp.bfloat16
LANES = 128
PIVOTS = 4
SMALL = pltpu.CompilerParams(vmem_limit_bytes=20 * 2**20)
VMEM = pl.BlockSpec(memory_space=pltpu.VMEM)


def dot(a, b, dims, precision=HIGHEST):
    return lax.dot_general(a, b, ((dims[:1], dims[1:]), ((), ())), precision=precision, preferred_element_type=F32)


def halves(a):
    high = a.astype(BF16)
    return high, (a - high.astype(F32)).astype(BF16)


def dot3(a, b, dims):
    (ah, al), (bh, bl) = a, b
    return dot(ah, bh, dims, None) + (dot(ah, bl, dims, None) + dot(al, bh, dims, None))


def packs(n, batch):
    return batch == LANES * 3 // 2 and n % 16 == 0


def pack(a):
    n, batch = a.shape
    if not packs(n, batch):
        return a
    tail = a[:, LANES:]
    return jnp.concatenate([a[:, :LANES], jnp.concatenate([tail[: n // 2], tail[n // 2 :]], axis=1)])


def unpack(a, n, batch):
    if not packs(n, batch):
        return a
    tail = a[n:]
    side = LANES // 2
    return jnp.concatenate([a[:n], jnp.concatenate([tail[:, :side], tail[:, side:]])], axis=1)


def inverse_kernel(first, last, s_ref, o_ref):
    n, width = o_ref.shape
    lane = lax.broadcasted_iota(jnp.int32, (1, width), 1)
    sub = lax.broadcasted_iota(jnp.int32, (n, 1), 0)
    if first == 0:
        s = s_ref[...]
        if len(s.shape) == 3:
            s = jnp.concatenate([unpack(s_ref[i], n // 2, n) for i in range(2)])
        if width > n:
            o_ref[:, n:] = jnp.zeros((n, width - n), F32)
        o_ref[:, :n] = 0.5 * (s + s.T)
        o_ref[...] += jnp.where(sub == lane, 1.0, 0.0)
    else:
        o_ref[...] = s_ref[...]

    def step(t, _):
        at = t * PIVOTS
        a = o_ref[...]
        hits = [lane == at + b for b in range(PIVOTS)]
        rows = [o_ref[pl.ds(at + b, 1), :] for b in range(PIVOTS)]
        p = [[jnp.sum(jnp.where(h, r, 0.0), axis=1, keepdims=True) for h in hits] for r in rows]
        cols = [jnp.sum(jnp.where(h, a, 0.0), axis=1, keepdims=True) for h in hits]
        for i in range(PIVOTS):
            inv = 1.0 / p[i][i]
            scaled = [inv if j == i else p[i][j] * inv for j in range(PIVOTS)]
            for o in range(PIVOTS):
                if o != i:
                    f = p[o][i]
                    p[o] = [-f * inv if j == i else p[o][j] - f * scaled[j] for j in range(PIVOTS)]
            p[i] = scaled
        in_lanes = (lane >= at) & (lane < at + PIVOTS)
        in_rows = (sub >= at) & (sub < at + PIVOTS)
        rows = [jnp.where(in_lanes, jnp.where(h, 1.0, 0.0), r) for h, r in zip(hits, rows)]
        out = jnp.where(in_rows | in_lanes, 0.0, a)
        for i in range(PIVOTS):
            new = p[i][0] * rows[0]
            for j in range(1, PIVOTS):
                new = new + p[i][j] * rows[j]
            out = out - jnp.where(in_rows, jnp.where(sub == at + i, -1.0, 0.0), cols[i]) * new
        o_ref[...] = out
        return 0

    lax.fori_loop(first, last, step, 0)


def eliminated(a, n, first, last):
    width = -(-n // LANES) * LANES
    return pl.pallas_call(
        functools.partial(inverse_kernel, first, last),
        out_shape=jax.ShapeDtypeStruct((n, width), F32),
        in_specs=[VMEM],
        out_specs=VMEM,
        compiler_params=SMALL,
        cost_estimate=pl.CostEstimate(flops=2 * n**3, bytes_accessed=8 * n * n, transcendentals=0),
        name="inverse",
    )(a)


def place_kernel(n, place, *refs):
    *piece_refs, high_ref, low_ref = refs
    for i, ref in enumerate(piece_refs):
        at = place[0] ^ i
        high_ref[at], low_ref[at] = halves(unpack(ref[...], n, high_ref.shape[2]))


def placed_halves(pieces, place, n, batch):
    shape = jax.ShapeDtypeStruct((len(pieces), n, batch), BF16)
    return pl.pallas_call(
        functools.partial(place_kernel, n),
        out_shape=(shape, shape),
        grid_spec=pltpu.PrefetchScalarGridSpec(
            num_scalar_prefetch=1, grid=(), in_specs=[VMEM] * len(pieces), out_specs=(VMEM, VMEM)
        ),
        compiler_params=SMALL,
        name="place",
    )(place, *pieces)


def product_kernel(a_ref, b_ref, o_ref):
    o_ref[...] = dot3(halves(a_ref[...]), halves(b_ref[...]), (1, 0))


def product_add_kernel(a_ref, b_ref, c_ref, o_ref):
    o_ref[...] = c_ref[...] + dot3(halves(a_ref[...]), halves(b_ref[...]), (1, 0))


def product(a, b, c=None):
    shape = a.shape[0], b.shape[1]
    return pl.pallas_call(
        product_kernel if c is None else product_add_kernel,
        out_shape=jax.ShapeDtypeStruct(shape, F32),
        in_specs=[VMEM] * (2 if c is None else 3),
        out_specs=VMEM,
        compiler_params=SMALL,
        name="product",
    )(*((a, b) if c is None else (a, b, c)))


def inner_kernel(n, batch, *refs):
    *in_refs, o_ref = refs
    half = len(in_refs) // 2
    inner = 0.0
    for u_ref, x_ref in zip(in_refs[:half], in_refs[half:]):
        inner = inner + dot(unpack(u_ref[...], n, batch), unpack(x_ref[...], n, batch), (0, 0))
    for i in range(2):
        o_ref[i] = pack(inner[i * batch // 2 : (i + 1) * batch // 2])


def inner_of(u, x, n, batch):
    return pl.pallas_call(
        functools.partial(inner_kernel, n, batch),
        out_shape=jax.ShapeDtypeStruct((2, batch * batch // 2 // LANES, LANES), F32),
        in_specs=[VMEM] * (2 * len(u)),
        out_specs=VMEM,
        compiler_params=SMALL,
        name="inner",
    )(*u, *x)


def terms_kernel(n, streams, e, group, place, cov_ref, high_ref, low_ref, o_ref, *scratch):
    pieces, _, batch = high_ref.shape
    packed = n * batch // LANES
    count = o_ref.shape[0] // packed
    at = [pl.ds(pl.multiple_of(((place[2] ^ e) * pieces + (place[1] ^ d)) * n, 8), n) for d in group]
    if streams:
        read_ref, sems = scratch
        copies = [pltpu.make_async_copy(cov_ref.at[at[i], :], read_ref.at[i], sems.at[i]) for i in range(count)]
        for copy in copies:
            copy.start()
    x = [ref[...].reshape(pieces * n, batch) for ref in (high_ref, low_ref)]
    for i in range(count):
        if streams:
            copies[i].wait()
        rows = read_ref[i] if streams else cov_ref[at[i], :]
        o_ref[i * packed : (i + 1) * packed, :] = pack(dot3(halves(rows), x, (1, 0)))


def row_terms(covariance, x_high, x_low, place, e, group, n, streams):
    width, batch = covariance.shape[1], x_high.shape[2]
    count = len(group)
    return pl.pallas_call(
        functools.partial(terms_kernel, n, streams, e, tuple(group)),
        out_shape=jax.ShapeDtypeStruct((count * n * batch // LANES, LANES), F32),
        grid_spec=pltpu.PrefetchScalarGridSpec(
            num_scalar_prefetch=1,
            grid=(),
            in_specs=[pl.BlockSpec(memory_space=pl.ANY) if streams else VMEM, VMEM, VMEM],
            out_specs=VMEM,
            scratch_shapes=[pltpu.VMEM((count, n, width), F32), pltpu.SemaphoreType.DMA((count,))] if streams else [],
        ),
        compiler_params=pltpu.CompilerParams(vmem_limit_bytes=46 * 2**20) if streams else SMALL,
        cost_estimate=pl.CostEstimate(
            flops=6 * count * n * width * batch, bytes_accessed=4 * count * n * width, transcendentals=0
        ),
        name="terms",
    )(place, covariance, x_high, x_low)


def gain_kernel(n, place, inverse_ref, *refs):
    *group_refs, high_ref, low_ref, own_ref, uh_ref, ul_ref = refs
    batch = inverse_ref.shape[0]
    size = n * batch // LANES
    per = group_refs[0].shape[0] // size
    count = len(group_refs) * per
    for i in range(count):
        packed = group_refs[i // per][i % per * size : (i % per + 1) * size, :]
        at = place[1] ^ i
        uh_ref[at], ul_ref[at] = halves(unpack(packed, n, batch))
    inverse = halves(inverse_ref[:, :batch])
    u = [ref[...].reshape(count * n, batch) for ref in (uh_ref, ul_ref)]
    high_ref[...], low_ref[...] = halves(dot3(inverse, u, (1, 1)))
    own_ref[...] = dot3((uh_ref[place[0]], ul_ref[place[0]]), inverse, (1, 0))


def gain_of(inverse, groups, place, n):
    batch = inverse.shape[0]
    count = sum(a.shape[0] for a in groups) // (n * batch // LANES)
    shape = jax.ShapeDtypeStruct((batch, count * n), BF16)
    return pl.pallas_call(
        functools.partial(gain_kernel, n),
        out_shape=(shape, shape, jax.ShapeDtypeStruct((n, batch), F32)),
        grid_spec=pltpu.PrefetchScalarGridSpec(
            num_scalar_prefetch=1,
            grid=(),
            in_specs=[VMEM] * (1 + len(groups)),
            out_specs=(VMEM,) * 3,
            scratch_shapes=[pltpu.VMEM((count, n, batch), BF16)] * 2,
        ),
        compiler_params=SMALL,
        name="gain",
    )(place, inverse, *groups)


def update_kernel(n, place, cov_ref, high_ref, low_ref, *refs):
    *group_refs, o_ref, stage_ref, sems = refs
    batch = high_ref.shape[0]
    size = n * batch // LANES
    per = group_refs[0].shape[0] // size
    pieces = high_ref.shape[1] // n
    gain = high_ref[...], low_ref[...]
    copies = []
    for i in range(len(group_refs) * per):
        block = (place[2] ^ (i // pieces)) * pieces + (place[1] ^ (i % pieces))
        at = pl.ds(pl.multiple_of(block * n, 8), n)
        rows = halves(unpack(group_refs[i // per][i % per * size : (i % per + 1) * size, :], n, batch))
        stage_ref[i] = cov_ref[at, :] - dot3(rows, gain, (1, 0))
        copies.append(pltpu.make_async_copy(stage_ref.at[i], o_ref.at[at, :], sems.at[i]))
        copies[i].start()
    for copy in copies:
        copy.wait()


def updated(covariance, gain_high, gain_low, groups, place, n):
    count, width = covariance.shape[0] // n, covariance.shape[1]
    return pl.pallas_call(
        functools.partial(update_kernel, n),
        out_shape=jax.ShapeDtypeStruct(covariance.shape, F32),
        grid_spec=pltpu.PrefetchScalarGridSpec(
            num_scalar_prefetch=1,
            grid=(),
            in_specs=[VMEM] * (3 + len(groups)),
            out_specs=pl.BlockSpec(memory_space=pl.ANY),
            scratch_shapes=[pltpu.VMEM((count, n, width), F32), pltpu.SemaphoreType.DMA((count,))],
        ),
        compiler_params=SMALL,
        name="update",
    )(place, covariance, gain_high, gain_low, *groups)


def after(a, *others):
    return lax.optimization_barrier((a, *others))[0]


def program(nr, nc):
    k = nc // nr
    assert k == 2

    def swap(a, axis, mask):
        n = nr if axis == "row" else nc
        return lax.ppermute(a, axis, [(i, i ^ mask) for i in range(n)])

    def bits_of(n):
        return [1 << b for b in range(n.bit_length() - 1)]

    masks = bits_of(nr)

    def on_device(covariance, samples, labels, weights):
        row, col = lax.axis_index("row"), lax.axis_index("col")
        z, x = lax.div(col, k), lax.rem(col, k)
        place = jnp.stack([row, z, x]).astype(jnp.int32)
        batch, piece = samples.shape
        fits = packs(piece, batch)

        first_of = {m: (row & m) == 0 for m in masks}
        handed_to = {m: ((row ^ z) & m) != 0 for m in masks}

        def ordered(low, mine, other):
            return jnp.where(low, mine, other), jnp.where(low, other, mine)

        xt = pack(samples.T)
        size = xt.shape[0]
        x_by = {0: xt}
        for mask in reversed(masks):
            for d in list(x_by):
                x_by[d | mask] = swap(x_by[d], "row", mask)
        order = list(reversed(range(nr)))
        groups = [order[: nr // 2], order[nr // 2 :]]

        if fits:
            x_high, x_low = placed_halves([x_by[d] for d in range(nr)], place, piece, batch)
            placed = x_high

            def terms_of(e, group, x_high):
                return row_terms(covariance, x_high, x_low, place, e, group, piece, e == 1 and group is groups[0])
        else:
            placed = jnp.concatenate([x_by[0]] * nr)
            for d in range(nr):
                placed = lax.dynamic_update_slice_in_dim(placed, x_by[d], (row ^ d) * piece, 0)
            whole = dot(covariance, placed, (1, 0), HIGH)

            def terms_of(e, group, _):
                at = [((x ^ e) * nr + (z ^ d)) * piece for d in group]
                return jnp.concatenate([lax.dynamic_slice_in_dim(whole, i, piece, 0) for i in at])

        predicted = product(samples, weights) if fits else dot(samples, weights, (1, 0))
        sends = [("row", 1)] + [("col", m * k) for m in masks] + [("row", m) for m in masks[1:]] + [("col", 1)]

        def step_on(predicted, *others):
            axis, mask = sends.pop(0)
            if (axis, mask) == ("row", 1):
                n = predicted.shape[0] // 2
                low = first_of[mask]
                a, b = predicted[:n], predicted[n:]
                keep, give = jnp.where(low, a, b), jnp.where(low, b, a)
            else:
                keep = give = predicted
            got = swap(give, axis, mask)
            predicted = keep + got
            return tuple(lax.optimization_barrier((predicted, *others)))

        transposed = [
            (z_ * nc + k * r_ + x_, r_ * nc + k * z_ + x_) for r_ in range(nr) for z_ in range(nr) for x_ in range(k)
        ]
        x_piece = lax.ppermute(xt, ("row", "col"), transposed)
        (predicted,) = step_on(predicted)
        placed, first_of, handed_to = lax.optimization_barrier((placed, first_of, handed_to))
        made, sent, kept = [], [], []
        for i, group in enumerate(groups):
            made.append(terms_of(1, group, placed))
            sent.append(swap(made[i], "col", 1))
        for group in groups:
            kept.append(terms_of(0, group, placed))
        while sends[1][0] == "col":
            (predicted,) = step_on(predicted)
            predicted = after(predicted, made[1])
        (predicted,) = step_on(predicted)

        part = {}
        for group, a, b in zip(groups, kept, sent):
            for i, d in enumerate(group):
                part[d] = a[i * size : (i + 1) * size] + b[i * size : (i + 1) * size]
        for mask in masks:
            for d in sorted(part, reverse=True):
                if d & mask:
                    got = swap(part.pop(d), "col", mask * k)
                    part[d ^ mask] = part[d ^ mask] + got
        u_piece = part[0]
        x_piece = after(x_piece, kept[1])

        if fits:
            inner = inner_of([u_piece], [x_piece], piece, batch)
        else:
            inner = dot(u_piece, x_piece, (0, 0)).reshape(2, batch // 2, batch)
        low = first_of[1]
        inner = jnp.where(low, inner[0], inner[1]) + swap(jnp.where(low, inner[1], inner[0]), "row", 1)
        for mask in reversed(masks):
            hop = swap(inner, "col", mask * k)
            inner = inner + hop
            if mask == masks[-1]:
                u_piece = after(u_piece, inner)
        while sends:
            (predicted,) = step_on(predicted)
        for mask in masks[1:]:
            inner = inner + swap(inner, "row", mask)
        for mask in bits_of(k):
            inner = inner + swap(inner, "col", mask)
        inner = jnp.stack(ordered(low, inner, swap(inner, "row", 1)))
        if not fits:
            inner = inner.reshape(batch, batch)
        got = swap(predicted, "row", 1)
        predicted = jnp.concatenate(ordered(first_of[1], predicted, got))

        u_by = {0: u_piece}
        for d in range(1, nr):
            u_by[d] = swap(u_piece, "col", d * k)
        own = [jnp.concatenate([u_by[d] for d in range(nr // 2)])]
        peer = [swap(own[0], "col", 1)]

        def handed(a, mask):
            pairs = [
                (r_ * nc + c_, (r_ ^ mask) * nc + c_)
                for c_ in range(nc)
                for r_ in range(nr)
                if (r_ ^ (c_ // k)) & (2 * mask - 1) == 0
            ]
            return jnp.where(handed_to[mask], lax.ppermute(a, ("row", "col"), pairs), a)

        steps = batch // PIVOTS
        near = own[0]
        for mask in reversed(masks[1:]):
            near = handed(near, mask)
        inverse = eliminated(inner, batch, 0, steps // 3)
        inverse, near = lax.optimization_barrier((inverse, near))
        near = handed(near, 1)
        inverse = eliminated(inverse, batch, steps // 3, 2 * steps // 3)
        inverse, *far = lax.optimization_barrier((inverse, *(u_by[d] for d in range(nr // 2, nr))))
        own.append(jnp.concatenate(far))
        peer.append(swap(own[1], "col", 1))
        far = own[1]
        for mask in reversed(masks):
            far = handed(far, mask)
        inverse = eliminated(inverse, batch, 2 * steps // 3, steps)
        u_cols = [near, far]

        classes = lax.broadcasted_iota(jnp.int32, (batch, weights.shape[1]), 1)
        missed = (labels[:, None] == classes).astype(F32) - predicted
        if fits:
            gain_high, gain_low, gain_piece = gain_of(inverse, u_cols, place, piece)
            new_covariance = updated(covariance, gain_high, gain_low, own + peer, place, piece)
            new_weights = product(gain_piece, missed, weights)
        else:

            def in_order(pieces):
                joined = jnp.concatenate(pieces)
                out = joined
                for d in range(nr):
                    got = joined[d * piece : (d + 1) * piece]
                    out = lax.dynamic_update_slice_in_dim(out, got, (z ^ d) * piece, 0)
                return out

            gain = dot(in_order(u_cols), inverse[:, :batch], (1, 0))
            gain_piece = lax.dynamic_slice_in_dim(gain, row * piece, piece, 0)
            u_rows = jnp.concatenate(ordered(x == 0, in_order(own), in_order(peer)))
            new_covariance = covariance - dot(u_rows, gain, (1, 1), HIGH)
            new_weights = weights + dot(gain_piece, missed, (1, 0))
        return new_covariance, new_weights

    return on_device


def solution(mesh):
    on_device = program(mesh.shape["row"], mesh.shape["col"])

    return jax.shard_map(
        on_device,
        mesh=mesh,
        in_specs=(P("row", "col"), P(None, ("col", "row")), P(), P(("col", "row"), None)),
        out_specs=(P("row", "col"), P(("col", "row"), None)),
        check_vma=False,
    )
```
